32 devices in a mesh: row: 4 (over y, x), col: 8 (over z, core).
Axes of the slice: x: 2, y: 2, z: 4, core: 2. Of those that a mesh axis runs over, the one named last changes fastest.
Arguments:
- inputs: bfloat16 [2, 8192, 2048], P(None, 'row', 'col'), may hold values from -8 to 8
- piece_starts: int32 [2, 8, 2], P(None, 'col'), may hold values from 0 to 768, as said below
- first_gain: float32 [2048], P('col'), may hold values from 0.1 to 1.9
- first_shift: float32 [2048], P('col'), may hold values from -1.75 to 1.75
- second_gain: float32 [2048], P('col'), may hold values from 0.1 to 1.9
- second_shift: float32 [2048], P('col'), may hold values from -1.75 to 1.75
- merged_weight: bfloat16 [2048, 6144], P('col', 'row'), may hold values from -0.125 to 0.125
- merged_bias: float32 [6144], P('row'), may hold values from -1.75 to 1.75
- output_weight: bfloat16 [2048, 2048], P('row', 'col'), may hold values from -1 to 1
- output_bias: float32 [2048], P('col'), may hold values from -1.75 to 1.75
- expand_weight: bfloat16 [2048, 8192], P('col', 'row'), may hold values from -0.125 to 0.125
- expand_bias: float32 [8192], P('row'), may hold values from -1.75 to 1.75
- reduce_weight: bfloat16 [8192, 2048], P('row', 'col'), may hold values from -0.0625 to 0.0625
- reduce_bias: float32 [2048], P('col'), may hold values from -1.75 to 1.75
- cotangent: bfloat16 [2, 8192, 2048], P(None, 'row', 'col'), may hold values from -8 to 8
Outputs:
- result: bfloat16 [2, 8192, 2048], P(None, 'row', 'col')
- input_grad: float32 [2, 8192, 2048], P(None, 'row', 'col')
- first_gain_grad: float32 [2048], P('col')
- first_shift_grad: float32 [2048], P('col')
- second_gain_grad: float32 [2048], P('col')
- second_shift_grad: float32 [2048], P('col')
- merged_weight_grad: float32 [2048, 6144], P('col', 'row')
- merged_bias_grad: float32 [6144], P('row')
- output_weight_grad: float32 [2048, 2048], P('row', 'col')
- output_bias_grad: float32 [2048], P('col')
- expand_weight_grad: float32 [2048, 8192], P('col', 'row')
- expand_bias_grad: float32 [8192], P('row')
- reduce_weight_grad: float32 [8192, 2048], P('row', 'col')
- reduce_bias_grad: float32 [2048], P('col')
The draws below stay inside these ranges and needn't reach their ends.
Inputs may be any that keep to these rules, and one draw needn't show every extreme that they name: `piece_starts`: piece k of a sequence starts between k * 512 and (k + 1) * 512 - 256, so pieces never intersect; in every draw some piece starts at 0 and some at 768.
All inputs are finite; a program needn't handle non-finite values.
Results may differ from the reference program's by a relative error of at most 0.01.
Values may be sent and summed in bfloat16 or wider, within the bound.
A program may use at most 512 MiB of HBM per device.

```python
import math
import jax
import jax.numpy as jnp
from jax import lax

D = 2048
HEADS = 8
HEAD = 256
FF = 8192
ROT = 64
L = 1024
PIECE = 256
PIECES = 2
MICRO = 2
SEQS_MB = 8
MB_TOK = 8192


def draw_inputs(key, part):
    base_key, scale_key = jax.random.split(key, 2)
    feature = jnp.arange(D, dtype=jnp.float32) / D
    column_scale = 0.6 * jnp.power(3.0, feature) * jax.random.uniform(scale_key, (D,), minval=0.7, maxval=1.3)
    values = jax.random.normal(base_key, (MICRO, MB_TOK, D)) * column_scale
    return jnp.clip(values, -8.0, 8.0).astype(jnp.bfloat16)


def draw_cotangent(key, part):
    base_key, scale_key = jax.random.split(jax.random.fold_in(key, 11), 2)
    token = jnp.arange(MB_TOK, dtype=jnp.float32) / MB_TOK
    row_scale = 0.6 * jnp.power(3.0, token)[None, :, None] * jax.random.uniform(scale_key, (MICRO, MB_TOK, 1), minval=0.7, maxval=1.3)
    values = jax.random.normal(base_key, (MICRO, MB_TOK, D)) * row_scale
    return jnp.clip(values, -8.0, 8.0).astype(jnp.bfloat16)


def draw_piece_starts(key, part):
    offset_key, first_key, last_key = jax.random.split(jax.random.fold_in(key, 23), 3)
    slot_len = L // PIECES
    seq_total = MICRO * SEQS_MB
    offsets = jax.random.randint(offset_key, (seq_total, PIECES), 0, slot_len - PIECE + 1)
    first_seq = jax.random.randint(first_key, (), 0, seq_total)
    last_seq = jax.random.randint(last_key, (), 0, seq_total)
    offsets = offsets.at[first_seq, 0].set(0)
    offsets = offsets.at[last_seq, PIECES - 1].set(slot_len - PIECE)
    bases = jnp.arange(PIECES, dtype=jnp.int32) * slot_len
    return (offsets + bases[None, :]).astype(jnp.int32).reshape(MICRO, SEQS_MB, PIECES)


def steps_of(own_key, extent, cuts, least, high):
    loudness, own = 1.0, jax.random.fold_in(own_key, 6)
    for position, parts in cuts:
        steps = jnp.exp(jax.random.uniform(jax.random.fold_in(own, position), (parts,), jnp.float32, least / len(cuts), high / len(cuts)))
        loudness = loudness * jnp.repeat(steps, extent[position] // parts).reshape([-1 if axis == position else 1 for axis in range(len(extent))])
    return loudness


def noise(key, extent, scale, most, cuts=(), kind=jnp.bfloat16):
    values = scale * jax.random.normal(key, extent, jnp.float32)
    if cuts:
        values = values * steps_of(key, extent, cuts, -0.22, 0.18)
    return jnp.clip(values, -most, most).astype(kind)


def setup_inputs(seed: int = 0) -> dict:
    keys = jax.random.split(jax.random.key(seed), 16)
    inputs = draw_inputs(jax.random.fold_in(keys[15], 71), 0)
    piece_starts = draw_piece_starts(jax.random.fold_in(keys[15], 71), 0)
    first_gain = jnp.clip(1.0 + 0.18 * jax.random.normal(keys[2], (D,), jnp.float32), 0.1, 1.9)
    first_shift = noise(keys[3], (D,), 0.3, 1.75, ((0, 8),), jnp.float32)
    second_gain = jnp.clip(1.0 + 0.18 * jax.random.normal(keys[4], (D,), jnp.float32), 0.1, 1.9)
    second_shift = noise(keys[5], (D,), 0.3, 1.75, ((0, 8),), jnp.float32)
    merged_weight = noise(keys[6], (D, 3 * D), D ** -0.5, 0.125, ((0, 8), (1, 4)))
    merged_bias = noise(keys[7], (3 * D,), 0.3, 1.75, ((0, 4),), jnp.float32)
    output_weight = noise(keys[8], (D, D), (D // 64) ** -0.5, 1.0, ((0, 4), (1, 8)))
    output_bias = noise(keys[9], (D,), 0.3, 1.75, ((0, 8),), jnp.float32)
    expand_weight = noise(keys[10], (D, FF), D ** -0.5, 0.125, ((0, 8), (1, 4)))
    expand_bias = noise(keys[11], (FF,), 0.3, 1.75, ((0, 4),), jnp.float32)
    reduce_weight = noise(keys[12], (FF, D), FF ** -0.5, 0.0625, ((0, 4), (1, 8)))
    reduce_bias = noise(keys[13], (D,), 0.3, 1.75, ((0, 8),), jnp.float32)
    cotangent = draw_cotangent(jax.random.fold_in(keys[15], 71), 0)
    return dict(inputs=inputs, piece_starts=piece_starts, first_gain=first_gain, first_shift=first_shift, second_gain=second_gain, second_shift=second_shift, merged_weight=merged_weight, merged_bias=merged_bias, output_weight=output_weight, output_bias=output_bias, expand_weight=expand_weight, expand_bias=expand_bias, reduce_weight=reduce_weight, reduce_bias=reduce_bias, cotangent=cotangent)


@jax.custom_vjp
def low(v):
    return lax.optimization_barrier(v.astype(jnp.bfloat16)).astype(jnp.float32)

@jax.custom_vjp
def low_back(v):
    return v

def low_keep(v):
    return (low(v), None)

def low_pass(kept, grad):
    return (grad,)

def back_keep(v):
    return (v, None)

def back_low(kept, grad):
    return (low(grad),)
low.defvjp(low_keep, low_pass)
low_back.defvjp(back_keep, back_low)
norm_eps = 1e-05
theta_base = 10000.0

def wide_dot(left, right):
    return jnp.einsum('gld,de->gle', left, right, precision=lax.Precision.HIGHEST)

def rotate_tail(values, positions):
    half_dims = ROT // 2
    freq_steps = jnp.arange(half_dims, dtype=jnp.float32)
    inverse = jnp.power(theta_base, -(2.0 * freq_steps) / ROT)
    angles = positions.astype(jnp.float32)[:, None] * inverse[None, :]
    cosine = jnp.cos(angles)[None, :, None, :]
    sine_table = jnp.sin(angles)[None, :, None, :]
    leading = values[..., :half_dims]
    trailing = values[..., half_dims:ROT]
    return jnp.concatenate([leading * cosine - trailing * sine_table, trailing * cosine + leading * sine_table, values[..., ROT:]], axis=-1)

def layer_group(group_inputs, group_starts, params):
    first_gain, first_shift, second_gain, second_shift, merged_weight, merged_bias, output_weight, output_bias, expand_weight, expand_bias, reduce_weight, reduce_bias = params
    group_size = group_inputs.shape[0]
    center = lax.optimization_barrier(jnp.mean(group_inputs, axis=-1, keepdims=True))
    spread = lax.optimization_barrier(jnp.mean((group_inputs - center) ** 2, axis=-1, keepdims=True))
    normed = (group_inputs - center) * lax.rsqrt(spread + norm_eps)
    attend_in = low(normed * first_gain + first_shift)
    expand_in = low(normed * second_gain + second_shift)
    merged_all = low_back(wide_dot(attend_in, merged_weight) + merged_bias).reshape(group_size, L, HEADS, 3, HEAD)
    token_pos = jnp.arange(L, dtype=jnp.int32)
    queries = low(rotate_tail(merged_all[:, :, :, 0, :], token_pos))
    keys_all = low(rotate_tail(merged_all[:, :, :, 1, :], token_pos))
    values = low(merged_all[:, :, :, 2, :])
    scores = low_back(jnp.einsum('gqhd,gkhd->ghqk', queries, keys_all, precision=lax.Precision.HIGHEST) * HEAD ** (-0.5))
    causal = token_pos[None, :] <= token_pos[:, None]
    inside = (token_pos[None, None, :] >= group_starts[:, :, None]) & (token_pos[None, None, :] < group_starts[:, :, None] + PIECE)
    same_piece = jnp.any(inside[:, :, :, None] & inside[:, :, None, :], axis=1)
    visible = causal[None, :, :] | same_piece
    scores = jnp.where(visible[:, None, :, :], scores, -jnp.inf)
    prob_table = low(jax.nn.softmax(scores, axis=-1))
    head_mix = low(low_back(jnp.einsum('ghqk,gkhd->gqhd', prob_table, values, precision=lax.Precision.HIGHEST))).reshape(group_size, L, D)
    attn_branch = wide_dot(head_mix, output_weight) + output_bias
    expand_pre = low_back(wide_dot(expand_in, expand_weight) + expand_bias)
    activated = low(jax.nn.gelu(expand_pre, approximate=False))
    ffn_branch = wide_dot(activated, reduce_weight) + reduce_bias
    return group_inputs + attn_branch + ffn_branch

def reference(inputs, piece_starts, first_gain, first_shift, second_gain, second_shift, merged_weight, merged_bias, output_weight, output_bias, expand_weight, expand_bias, reduce_weight, reduce_bias, cotangent):
    seq_total = inputs.shape[0] * inputs.shape[1] // L
    group_size = math.gcd(seq_total, max(1, 4096 // L))
    group_count = seq_total // group_size
    seq_inputs = inputs.astype(jnp.float32).reshape(group_count, group_size, L, D)
    seq_starts = piece_starts.reshape(group_count, group_size, PIECES).astype(jnp.int32)
    params = (first_gain.astype(jnp.float32), first_shift.astype(jnp.float32), second_gain.astype(jnp.float32), second_shift.astype(jnp.float32), merged_weight.astype(jnp.float32), merged_bias.astype(jnp.float32), output_weight.astype(jnp.float32), output_bias.astype(jnp.float32), expand_weight.astype(jnp.float32), expand_bias.astype(jnp.float32), reduce_weight.astype(jnp.float32), reduce_bias.astype(jnp.float32))
    layer_step = jax.checkpoint(layer_group)

    def forward(all_inputs, all_params):

        def scan_step(scan_carry, scan_item):
            return (scan_carry, layer_step(scan_item[0], scan_item[1], all_params))
        return lax.scan(scan_step, jnp.zeros((), jnp.float32), (all_inputs, seq_starts))[1]
    outputs, pullback = jax.vjp(forward, seq_inputs, params)
    grad_inputs, grad_params = pullback(cotangent.astype(jnp.float32).reshape(outputs.shape))
    result = outputs.reshape(inputs.shape).astype(jnp.bfloat16)
    return (result, grad_inputs.reshape(inputs.shape), grad_params[0], grad_params[1], grad_params[2], grad_params[3], grad_params[4], grad_params[5], grad_params[6], grad_params[7], grad_params[8], grad_params[9], grad_params[10], grad_params[11])
```

```python
import jax
import jax.numpy as jnp
from jax import lax
from jax.sharding import PartitionSpec as P

D = 2048
HEAD = 256
ROT = 64
L = 1024
PIECE = 256
HALF_SEQ = 512

norm_eps = 1e-05
theta_base = 10000.0
BF = jnp.bfloat16
F32 = jnp.float32


def mm(left, right):
    return jnp.dot(left, right, preferred_element_type=F32)


def contract_last(left, right):
    return lax.dot_general(left, right, (((1,), (1,)), ((), ())), preferred_element_type=F32)


def contract_first(left, right):
    return lax.dot_general(left, right, (((0,), (0,)), ((), ())), preferred_element_type=F32)


def rotary_tables():
    half_dims = ROT // 2
    freq_steps = jnp.arange(half_dims, dtype=F32)
    inverse = jnp.power(theta_base, -(2.0 * freq_steps) / ROT)
    angles = jnp.arange(L, dtype=jnp.int32).astype(F32)[:, None] * inverse[None, :]
    return jnp.cos(angles), jnp.sin(angles)


def turn(segment, cosine, sine):
    half_dims = ROT // 2
    leading = segment[:, :half_dims]
    trailing = segment[:, half_dims:ROT]
    return jnp.concatenate(
        [leading * cosine - trailing * sine, trailing * cosine + leading * sine, segment[:, ROT:]],
        axis=1,
    )


def visible_mask(query_pos, key_pos, seq_bounds):
    allowed = key_pos[None, :] <= query_pos[:, None]
    for piece_index in range(seq_bounds.shape[0]):
        lower = seq_bounds[piece_index]
        inside_query = (query_pos >= lower) & (query_pos < lower + PIECE)
        inside_key = (key_pos >= lower) & (key_pos < lower + PIECE)
        allowed = allowed | inside_query[:, None] & inside_key[None, :]
    return allowed


def body(
    inputs,
    piece_starts,
    first_gain,
    first_shift,
    second_gain,
    second_shift,
    merged_weight,
    merged_bias,
    output_weight,
    output_bias,
    expand_weight,
    expand_bias,
    reduce_weight,
    reduce_bias,
    cotangent,
):
    rows = lax.axis_size("row")
    cols = lax.axis_size("col")
    micro, own_tokens, width = inputs.shape
    per_row = own_tokens // L
    part = L // rows
    heads = merged_weight.shape[1] // (3 * HEAD)
    scale = HEAD ** (-0.5)
    cosine, sine = rotary_tables()

    def to_rows(block):
        b = block.reshape(micro, per_row, rows, part, width).transpose(2, 1, 0, 3, 4)
        b = lax.all_to_all(b, "row", split_axis=0, concat_axis=0, tiled=True)
        b = b.reshape(rows * per_row, micro, part, width)
        b = lax.all_to_all(b, "col", split_axis=0, concat_axis=0, tiled=True)
        return b.transpose(1, 2, 0, 3).reshape(micro, part, cols * width)

    def from_rows(block):
        b = block.reshape(micro, part, cols, width).transpose(2, 0, 1, 3)
        b = lax.all_to_all(b, "col", split_axis=0, concat_axis=0, tiled=True)
        b = b.reshape(rows, per_row, micro, part, width)
        b = lax.all_to_all(b, "row", split_axis=0, concat_axis=0, tiled=True)
        return b.transpose(2, 1, 0, 3, 4).reshape(micro, own_tokens, width)

    def whole_seq(part_rows):
        return lax.all_gather(part_rows, "row", axis=1, tiled=True).reshape(micro * L, D)

    def norm(block):
        block = block.astype(F32)
        center = jnp.mean(block, axis=-1, keepdims=True)
        spread = jnp.mean((block - center) ** 2, axis=-1, keepdims=True)
        inverse_std = lax.rsqrt(spread + norm_eps)
        return (block - center) * inverse_std, inverse_std

    gains = lax.all_gather(
        jnp.stack([first_gain, first_shift, second_gain, second_shift]), "col", axis=1, tiled=True
    )
    x_part = to_rows(inputs)
    x_seq = whole_seq(x_part)
    merged_w = lax.all_gather(merged_weight, "col", axis=0, tiled=True)
    expand_w = lax.all_gather(expand_weight, "col", axis=0, tiled=True)
    cot_part = to_rows(cotangent)
    cot_seq = whole_seq(cot_part)
    reduce_w = lax.all_gather(reduce_weight, "col", axis=1, tiled=True)
    output_w = lax.all_gather(output_weight, "col", axis=1, tiled=True)

    normed, _ = norm(x_seq)
    attend_in = (normed * gains[0] + gains[1]).astype(BF)
    expand_in = (normed * gains[2] + gains[3]).astype(BF)

    expand_pre = mm(expand_in, expand_w) + expand_bias
    activated = jax.nn.gelu(expand_pre, approximate=False).astype(BF)
    grad_act = contract_last(cot_seq, reduce_w)
    gelu = lambda v: jax.nn.gelu(v, approximate=False)
    grad_pre = jax.vjp(gelu, expand_pre)[1](grad_act)[0].astype(BF)

    def scatter_weight(grad):
        return lax.psum_scatter(grad.astype(BF), "col", scatter_dimension=0, tiled=True).astype(F32)

    reduce_grad = scatter_weight(contract_first(cot_seq, activated)).T
    expand_grad = scatter_weight(contract_first(expand_in, grad_pre))

    merged_pre = mm(attend_in, merged_w) + merged_bias
    grad_mix = contract_last(cot_seq, output_w).astype(BF)
    token_pos = jnp.arange(L, dtype=jnp.int32)
    mixes = []
    grads = []
    for m in range(micro):
        bounds = piece_starts[m, 0]
        seq_mix = []
        seq_grads = []
        for h in range(heads):
            rows_m = slice(m * L, (m + 1) * L)
            base = 3 * h * HEAD
            query = turn(merged_pre[rows_m, base : base + HEAD], cosine, sine).astype(BF)
            key = turn(merged_pre[rows_m, base + HEAD : base + 2 * HEAD], cosine, sine).astype(BF)
            value = merged_pre[rows_m, base + 2 * HEAD : base + 3 * HEAD].astype(BF)
            gm = grad_mix[rows_m, h * HEAD : (h + 1) * HEAD]
            outs = []
            gq = []
            gk = jnp.zeros((L, HEAD), F32)
            gv = jnp.zeros((L, HEAD), F32)
            for first in range(0, L, HALF_SEQ):
                last = first + HALF_SEQ
                q, k, v, g = query[first:last], key[:last], value[:last], gm[first:last]
                mask = visible_mask(token_pos[first:last], token_pos[:last], bounds)
                scores = jnp.where(mask, contract_last(q, k) * scale, -jnp.inf)
                top = jnp.max(scores, axis=1, keepdims=True)
                es = jnp.exp(scores - top)
                probs = es / jnp.sum(es, axis=1, keepdims=True)
                pb = probs.astype(BF)
                outs.append(mm(pb, v).astype(BF))
                gp = contract_last(g, v)
                delta = jnp.sum(gp * probs, axis=1, keepdims=True)
                gs = (probs * (gp - delta)).astype(BF)
                gq.append(mm(gs, k) * scale)
                pad = ((0, L - last), (0, 0))
                gk = gk + jnp.pad(contract_first(gs, q) * scale, pad)
                gv = gv + jnp.pad(contract_first(pb, g), pad)
            seq_mix.append(jnp.concatenate(outs, axis=0))
            gq = jnp.concatenate(gq, axis=0)
            seq_grads += [turn(gq, cosine, -sine), turn(gk, cosine, -sine), gv]
        mixes.append(jnp.concatenate(seq_mix, axis=1))
        grads.append(jnp.concatenate(seq_grads, axis=1).astype(BF))
    mix = jnp.concatenate(mixes, axis=0)
    grad_merged = jnp.concatenate(grads, axis=0)

    branch = mm(mix, output_w) + mm(activated, reduce_w)
    branch = branch.astype(BF).reshape(micro, L, D)
    branch = lax.psum_scatter(branch, "row", scatter_dimension=1, tiled=True)
    branch = from_rows(branch)
    result = inputs.astype(F32) + branch.astype(F32) + output_bias + reduce_bias
    result = result.astype(BF)

    output_grad = scatter_weight(contract_first(cot_seq, mix)).T
    merged_grad = scatter_weight(contract_first(attend_in, grad_merged))

    grad_first = contract_last(grad_merged, merged_w)
    grad_second = contract_last(grad_pre, expand_w)
    norm_sums = jnp.stack(
        [
            jnp.sum(grad_first * normed, axis=0),
            jnp.sum(grad_first, axis=0),
            jnp.sum(grad_second * normed, axis=0),
            jnp.sum(grad_second, axis=0),
        ]
    )
    grad_hat = (grad_first * gains[0] + grad_second * gains[2]).astype(BF).reshape(micro, L, D)
    grad_hat = lax.psum_scatter(grad_hat, "row", scatter_dimension=1, tiled=True).astype(F32)
    part_normed, part_inverse = norm(x_part)
    norm_part = part_inverse * (
        grad_hat
        - jnp.mean(grad_hat, axis=-1, keepdims=True)
        - part_normed * jnp.mean(grad_hat * part_normed, axis=-1, keepdims=True)
    )
    input_grad = cotangent.astype(F32) + from_rows(norm_part.astype(BF)).astype(F32)

    norm_sums = lax.psum(lax.psum_scatter(norm_sums, "col", scatter_dimension=1, tiled=True), "row")
    merged_b = lax.psum(jnp.sum(grad_merged.astype(F32), axis=0), "col")
    expand_b = lax.psum(jnp.sum(grad_pre.astype(F32), axis=0), "col")
    shift_b = lax.psum(jnp.sum(cotangent.astype(F32), axis=(0, 1)), "row")
    return (
        result,
        input_grad,
        norm_sums[0],
        norm_sums[1],
        norm_sums[2],
        norm_sums[3],
        merged_grad,
        merged_b,
        output_grad,
        shift_b,
        expand_grad,
        expand_b,
        reduce_grad,
        shift_b,
    )


def solution(mesh):
    in_specs = (
        P(None, "row", "col"),
        P(None, "col", None),
        P("col"),
        P("col"),
        P("col"),
        P("col"),
        P("col", "row"),
        P("row"),
        P("row", "col"),
        P("col"),
        P("col", "row"),
        P("row"),
        P("row", "col"),
        P("col"),
        P(None, "row", "col"),
    )
    out_specs = (
        P(None, "row", "col"),
        P(None, "row", "col"),
        P("col"),
        P("col"),
        P("col"),
        P("col"),
        P("col", "row"),
        P("row"),
        P("row", "col"),
        P("col"),
        P("col", "row"),
        P("row"),
        P("row", "col"),
        P("col"),
    )
    return jax.shard_map(body, mesh=mesh, in_specs=in_specs, out_specs=out_specs, check_vma=False)
```

```python
import functools

import jax
import jax.numpy as jnp
from jax import lax
from jax.experimental import pallas as pl
from jax.experimental.pallas import tpu as pltpu
from jax.sharding import PartitionSpec as P

D = 2048
HEAD = 256
ROT = 64
L = 1024
PIECE = 256
SPAN = 512

norm_eps = 1e-05
theta_base = 10000.0
BF = jnp.bfloat16
F32 = jnp.float32


def mm(left, right):
    return jnp.dot(left, right, preferred_element_type=F32)


def contract_last(left, right):
    return lax.dot_general(left, right, (((1,), (1,)), ((), ())), preferred_element_type=F32)


def contract_first(left, right):
    return lax.dot_general(left, right, (((0,), (0,)), ((), ())), preferred_element_type=F32)


def rotary_tables():
    half = ROT // 2
    freq_steps = jnp.arange(half, dtype=F32)
    inverse = jnp.power(theta_base, -(2.0 * freq_steps) / ROT)
    angles = jnp.arange(L, dtype=jnp.int32).astype(F32)[:, None] * inverse[None, :]
    cosine = jnp.cos(angles)
    sine = jnp.sin(angles)
    rest = 128 - ROT
    cos_table = jnp.concatenate([cosine, cosine, jnp.ones((L, rest), F32)], axis=1)
    sin_table = jnp.concatenate([-sine, sine, jnp.zeros((L, rest), F32)], axis=1)
    return cos_table, sin_table


def turn(block, cos, sin):
    half = ROT // 2
    head = block[:, :128]
    lane = lax.broadcasted_iota(jnp.int32, head.shape, 1)
    partner = jnp.where(lane < half, pltpu.roll(head, 128 - half, 1), pltpu.roll(head, half, 1))
    return jnp.concatenate([head * cos + partner * sin, block[:, 128:]], axis=1)


def attention_kernel(
    slot_ref, starts_ref, pre_ref, gm_ref, cos_ref, sin_ref,
    mix_ref, grad_ref, q_s, k_s, v_s, g_s, gk_s, gv_s, *, parts, part,
):
    m = pl.program_id(1)
    scale = HEAD ** (-0.5)
    for a in range(parts):
        rows = slice(a * part, (a + 1) * part)
        j = slot_ref[a]
        block = pre_ref[j, 0]
        cos, sin = cos_ref[rows], sin_ref[rows]
        q_s[rows] = turn(block[:, :HEAD], cos, sin).astype(BF)
        k_s[rows] = turn(block[:, HEAD : 2 * HEAD], cos, sin).astype(BF)
        v_s[rows] = block[:, 2 * HEAD :].astype(BF)
        g_s[rows] = gm_ref[j, 0]
    for first in range(0, L, SPAN):
        last = first + SPAN
        q, g = q_s[first:last], g_s[first:last]
        k, v = k_s[:last], v_s[:last]
        row = lax.broadcasted_iota(jnp.int32, (SPAN, 1), 0) + first
        limit = row
        for piece in range(2):
            low = starts_ref[2 * m + piece]
            limit = jnp.where((row >= low) & (row < low + PIECE), low + PIECE - 1, limit)
        column = lax.broadcasted_iota(jnp.int32, (SPAN, last), 1)
        scores = jnp.where(column <= limit, contract_last(q, k) * scale, -jnp.inf)
        top = jnp.max(scores, axis=1, keepdims=True)
        powers = jnp.exp(scores - top)
        probs = powers * (1.0 / jnp.sum(powers, axis=1, keepdims=True))
        pb = probs.astype(BF)
        mix = mm(pb, v).astype(BF)
        gp = contract_last(g, v)
        delta = jnp.sum(gp * probs, axis=1, keepdims=True)
        gs = (probs * (gp - delta)).astype(BF)
        gq = mm(gs, k) * scale
        gk = contract_first(gs, q)
        gv = contract_first(pb, g)
        if first == 0:
            gk_s[:last] = gk
            gv_s[:last] = gv
            gk_s[last:] = jnp.zeros((L - last, HEAD), F32)
            gv_s[last:] = jnp.zeros((L - last, HEAD), F32)
        else:
            gk_s[:last] += gk
            gv_s[:last] += gv
        for a in range(first // part, last // part):
            rows = slice(a * part - first, (a + 1) * part - first)
            table = slice(a * part, (a + 1) * part)
            j = slot_ref[a]
            mix_ref[j, 0] = mix[rows]
            grad_ref[j, 0, :, :HEAD] = turn(gq[rows], cos_ref[table], -sin_ref[table]).astype(BF)
    for a in range(parts):
        rows = slice(a * part, (a + 1) * part)
        j = slot_ref[a]
        gk = gk_s[rows] * scale
        grad_ref[j, 0, :, HEAD : 2 * HEAD] = turn(gk, cos_ref[rows], -sin_ref[rows]).astype(BF)
        grad_ref[j, 0, :, 2 * HEAD :] = gv_s[rows].astype(BF)


def attention(slots, starts, merged_pre, grad_mix, micro, parts):
    part = L // parts
    heads = merged_pre.shape[1] // (3 * HEAD)
    cos, sin = rotary_tables()
    pre = merged_pre.reshape(parts, micro, part, heads * 3 * HEAD)
    gm = grad_mix.reshape(parts, micro, part, heads * HEAD)
    spec = lambda w: pl.BlockSpec((parts, 1, part, w), lambda h, m, *_: (0, m, 0, h))
    table = pl.BlockSpec((L, 128), lambda h, m, *_: (0, 0))
    flops = heads * micro * 2 * 5 * L * L * HEAD * 3 // 4
    mix, grads = pl.pallas_call(
        functools.partial(attention_kernel, parts=parts, part=part),
        out_shape=(
            jax.ShapeDtypeStruct(gm.shape, BF),
            jax.ShapeDtypeStruct(pre.shape, BF),
        ),
        grid_spec=pltpu.PrefetchScalarGridSpec(
            num_scalar_prefetch=2,
            grid=(heads, micro),
            in_specs=[spec(3 * HEAD), spec(HEAD), table, table],
            out_specs=[spec(HEAD), spec(3 * HEAD)],
            scratch_shapes=[pltpu.VMEM((L, HEAD), BF)] * 4 + [pltpu.VMEM((L, HEAD), F32)] * 2,
        ),
        compiler_params=pltpu.CompilerParams(
            dimension_semantics=("arbitrary", "arbitrary"), vmem_limit_bytes=60 << 20
        ),
        cost_estimate=pl.CostEstimate(
            flops=2 * flops, bytes_accessed=pre.size * 6 + gm.size * 4, transcendentals=heads * micro * L * L
        ),
        name="attention",
    )(slots, starts, pre, gm, cos, sin)
    return mix.reshape(-1, heads * HEAD), grads.reshape(-1, heads * 3 * HEAD)


def after(value, *earlier):
    return lax.optimization_barrier((value,) + earlier)[0]


def ring_order(rows):
    if rows < 4:
        return list(range(rows))
    half = rows // 2
    return list(range(half)) + list(range(rows - 1, half - 1, -1))


def body(
    inputs,
    piece_starts,
    first_gain,
    first_shift,
    second_gain,
    second_shift,
    merged_weight,
    merged_bias,
    output_weight,
    output_bias,
    expand_weight,
    expand_bias,
    reduce_weight,
    reduce_bias,
    cotangent,
):
    rows = lax.axis_size("row")
    cols = lax.axis_size("col")
    micro, own_tokens, width = inputs.shape
    per_row = own_tokens // L
    part = L // rows
    block_rows = micro * part
    order = ring_order(rows)
    spot = [order.index(r) for r in range(rows)]
    ahead = [(order[i], order[(i + 1) % rows]) for i in range(rows)]
    behind = [(b, a) for a, b in ahead]
    me = lax.axis_index("row")
    my_spot = jnp.asarray(spot, jnp.int32)[me]
    slots = (jnp.asarray(spot, jnp.int32) - my_spot) % rows
    up = lambda v: lax.ppermute(v, "row", ahead)
    down = lambda v: lax.ppermute(v, "row", behind)

    def row_swap(pair):
        b = pair.reshape(2, micro, per_row, rows, part, width).transpose(3, 0, 2, 1, 4, 5)
        b = lax.all_to_all(b, "row", split_axis=0, concat_axis=0, tiled=True)
        b = b.reshape(rows, 2, per_row, block_rows, width)
        return (b[:, i].reshape(rows * per_row, block_rows, width) for i in range(2))

    def col_swap(b):
        return lax.all_to_all(b, "col", split_axis=0, concat_axis=0, tiled=True)

    def side_by_side(b):
        return b.transpose(1, 0, 2).reshape(block_rows, cols * width)

    def from_rows(block):
        b = block.reshape(block_rows, cols, width).transpose(1, 0, 2)
        b = lax.all_to_all(b, "col", split_axis=0, concat_axis=0, tiled=True)
        b = b.reshape(rows, per_row, micro, part, width)
        b = lax.all_to_all(b, "row", split_axis=0, concat_axis=0, tiled=True)
        return b.transpose(2, 1, 0, 3, 4).reshape(micro, own_tokens, width)

    def ring_gather(own):
        pieces = [None] * rows
        pieces[0] = own
        fore, back = own, own
        far = rows // 2
        cut = block_rows // 2
        for step in range(1, far):
            fore, back = up(fore), down(back)
            pieces[rows - step], pieces[step] = fore, back
        pieces[far] = jnp.concatenate([up(fore[:cut]), down(back[cut:])], axis=0)
        return jnp.concatenate(pieces, axis=0)

    def ring_scatter(total):
        chunk = lambda j: total[j * block_rows : (j + 1) * block_rows]
        far = rows // 2
        cut = block_rows // 2
        half_up, half_down = up(chunk(far)[:cut].astype(BF)), down(chunk(far)[cut:].astype(BF))
        fore = back = None
        for step in range(far - 1, 0, -1):
            a, b = chunk(step), chunk(rows - step)
            if fore is None:
                a = jnp.concatenate([a[:cut] + half_up.astype(F32), a[cut:]], axis=0)
                b = jnp.concatenate([b[:cut], b[cut:] + half_down.astype(F32)], axis=0)
            else:
                a, b = a + fore.astype(F32), b + back.astype(F32)
            fore, back = up(a.astype(BF)), down(b.astype(BF))
        return chunk(0) + fore.astype(F32) + back.astype(F32)

    def norm(block):
        block = block.astype(F32)
        center = jnp.mean(block, axis=-1, keepdims=True)
        spread = jnp.mean((block - center) ** 2, axis=-1, keepdims=True)
        inverse_std = lax.rsqrt(spread + norm_eps)
        return (block - center) * inverse_std, inverse_std

    def broadcast(value, axis, size):
        return lax.all_to_all(
            jnp.broadcast_to(value, (size,) + value.shape), axis, split_axis=0, concat_axis=0, tiled=True
        )

    gains = jnp.stack([first_gain, first_shift, second_gain, second_shift])
    gains = broadcast(gains, "col", cols).transpose(1, 0, 2).reshape(4, cols * width)
    expand_w = lax.all_gather(expand_weight, "col", axis=0, tiled=True)
    x_half, cot_half = row_swap(jnp.stack([inputs, cotangent]))
    reduce_w = lax.all_gather(after(reduce_weight, x_half), "col", axis=1, tiled=True)
    mixed_weight = jnp.concatenate([merged_weight, output_weight.T], axis=1)
    x_part = col_swap(after(x_half, gains))
    mixed_w = lax.all_gather(after(mixed_weight, x_part), "col", axis=0, tiled=True)
    merged_cols = merged_weight.shape[1]
    merged_w, output_wt = mixed_w[:, :merged_cols], mixed_w[:, merged_cols:]
    cot_part = col_swap(after(cot_half, x_part))
    x_part = side_by_side(x_part)
    x_seq = ring_gather(x_part)
    cot_part = side_by_side(after(cot_part, x_seq))
    cot_seq = ring_gather(cot_part)

    normed, _ = norm(x_seq)
    attend_in = (normed * gains[0] + gains[1]).astype(BF)
    expand_in = (normed * gains[2] + gains[3]).astype(BF)

    expand_pre = lax.optimization_barrier(mm(expand_in, expand_w) + expand_bias)
    phi_sum = 0.5 * (1.0 + lax.erf(expand_pre * (0.5 ** 0.5)))
    density = jnp.exp(-0.5 * expand_pre * expand_pre) * 0.3989422804014327
    activated = (expand_pre * phi_sum).astype(BF)
    slope = (phi_sum + expand_pre * density).astype(BF)
    activated, slope = lax.optimization_barrier((activated, slope))

    def scatter_weight(grad):
        return lax.psum_scatter(grad, "col", scatter_dimension=0, tiled=True).astype(F32)

    reduce_dot = contract_first(cot_seq, activated).astype(BF)
    reduce_grad = scatter_weight(reduce_dot).T
    grad_act = contract_last(after(cot_seq, reduce_dot), reduce_w)
    grad_pre = (grad_act * slope.astype(F32)).astype(BF)
    expand_b = jnp.sum(grad_pre.astype(F32), axis=0)
    expand_dot = contract_first(expand_in, grad_pre).astype(BF)
    expand_grad = scatter_weight(expand_dot)

    merged_pre = mm(after(attend_in, expand_dot), merged_w) + merged_bias
    grad_mix = mm(after(cot_seq, expand_dot), output_wt).astype(BF)
    mix, grad_merged = attention(
        slots, piece_starts.reshape(-1), merged_pre, grad_mix, micro, rows
    )
    attend_late, cot_late, mix_late = lax.optimization_barrier(
        (attend_in, cot_seq, mix, reduce_grad)
    )[:3]
    mixed_dot = jnp.concatenate(
        [
            contract_first(attend_late, grad_merged).astype(BF),
            contract_first(cot_late, mix_late).astype(BF),
        ],
        axis=1,
    )
    mixed_grad = scatter_weight(mixed_dot)
    merged_grad, output_grad = mixed_grad[:, :merged_cols], mixed_grad[:, merged_cols:].T

    mix, activated = after((mix, activated), mixed_dot)
    branch = contract_last(mix, output_wt) + mm(activated, reduce_w)
    grad_pre, grad_merged, branch = lax.optimization_barrier(
        (grad_pre, grad_merged, branch, expand_grad)
    )[:3]
    branch = from_rows(ring_scatter(branch).astype(BF))
    result = inputs.astype(F32) + branch.astype(F32) + output_bias + reduce_bias
    result = result.astype(BF)

    grad_first = contract_last(grad_merged, merged_w)
    grad_second = contract_last(grad_pre, expand_w)
    norm_sums = jnp.stack(
        [
            jnp.sum(grad_first * normed, axis=0),
            jnp.sum(grad_first, axis=0),
            jnp.sum(grad_second * normed, axis=0),
            jnp.sum(grad_second, axis=0),
        ]
    )
    grad_hat = ring_scatter(grad_first * gains[0] + grad_second * gains[2])
    part_normed, part_inverse = norm(x_part)
    norm_part = part_inverse * (
        grad_hat
        - jnp.mean(grad_hat, axis=-1, keepdims=True)
        - part_normed * jnp.mean(grad_hat * part_normed, axis=-1, keepdims=True)
    )
    input_grad = cotangent.astype(F32) + from_rows(norm_part.astype(BF)).astype(F32)

    merged_b = jnp.sum(grad_merged.astype(F32), axis=0)
    shift_b = jnp.sum(cotangent.astype(F32), axis=(0, 1))
    sums = jnp.concatenate(
        [
            norm_sums.reshape(4, cols, width).transpose(1, 0, 2).reshape(cols, 4 * width),
            jnp.broadcast_to(merged_b, (cols, merged_cols)),
            jnp.broadcast_to(expand_b, (cols, expand_b.shape[0])),
        ],
        axis=1,
    ).reshape(cols, -1, 128)
    sums = lax.all_to_all(sums, "col", split_axis=0, concat_axis=0, tiled=True)
    sums = jnp.sum(sums.reshape(cols, -1), axis=0)
    merged_b = sums[4 * width : 4 * width + merged_cols]
    expand_b = sums[4 * width + merged_cols :]
    tail = jnp.concatenate([sums[: 4 * width], shift_b]).reshape(-1, 128)
    tail = jnp.sum(broadcast(tail, "row", rows), axis=0).reshape(5, width)
    norm_sums, shift_b = tail[:4], tail[4]
    return (
        result,
        input_grad,
        norm_sums[0],
        norm_sums[1],
        norm_sums[2],
        norm_sums[3],
        merged_grad,
        merged_b,
        output_grad,
        shift_b,
        expand_grad,
        expand_b,
        reduce_grad,
        shift_b,
    )


def solution(mesh):
    in_specs = (
        P(None, "row", "col"),
        P(None, "col", None),
        P("col"),
        P("col"),
        P("col"),
        P("col"),
        P("col", "row"),
        P("row"),
        P("row", "col"),
        P("col"),
        P("col", "row"),
        P("row"),
        P("row", "col"),
        P("col"),
        P(None, "row", "col"),
    )
    out_specs = (
        P(None, "row", "col"),
        P(None, "row", "col"),
        P("col"),
        P("col"),
        P("col"),
        P("col"),
        P("col", "row"),
        P("row"),
        P("row", "col"),
        P("col"),
        P("col", "row"),
        P("row"),
        P("row", "col"),
        P("col"),
    )
    return jax.shard_map(body, mesh=mesh, in_specs=in_specs, out_specs=out_specs, check_vma=False)
```

```python
import functools

import jax
import jax.numpy as jnp
from jax import lax
from jax.experimental import pallas as pl
from jax.experimental.pallas import tpu as pltpu
from jax.sharding import PartitionSpec as P

D = 2048
HEAD = 256
ROT = 64
L = 1024
PIECE = 256
SPAN = 512

norm_eps = 1e-05
theta_base = 10000.0
BF = jnp.bfloat16
F32 = jnp.float32


def mm(left, right):
    return jnp.dot(left, right, preferred_element_type=F32)


def contract_last(left, right):
    return lax.dot_general(left, right, (((1,), (1,)), ((), ())), preferred_element_type=F32)


def contract_first(left, right):
    return lax.dot_general(left, right, (((0,), (0,)), ((), ())), preferred_element_type=F32)


def rotary_tables():
    half = ROT // 2
    freq_steps = jnp.arange(half, dtype=F32)
    inverse = jnp.power(theta_base, -(2.0 * freq_steps) / ROT)
    angles = jnp.arange(L, dtype=jnp.int32).astype(F32)[:, None] * inverse[None, :]
    cosine = jnp.cos(angles)
    sine = jnp.sin(angles)
    rest = 128 - ROT
    cos_table = jnp.concatenate([cosine, cosine, jnp.ones((L, rest), F32)], axis=1)
    sin_table = jnp.concatenate([-sine, sine, jnp.zeros((L, rest), F32)], axis=1)
    return cos_table, sin_table


def turn(block, cos, sin):
    half = ROT // 2
    head = block[:, :128]
    lane = lax.broadcasted_iota(jnp.int32, head.shape, 1)
    partner = jnp.where(lane < half, pltpu.roll(head, 128 - half, 1), pltpu.roll(head, half, 1))
    return jnp.concatenate([head * cos + partner * sin, block[:, 128:]], axis=1)


def attention_kernel(
    slot_ref, starts_ref, pre_ref, gm_ref, cos_ref, sin_ref,
    mix_ref, grad_ref, q_s, k_s, v_s, g_s, gk_s, gv_s, *, parts, part,
):
    m = pl.program_id(1)
    scale = HEAD ** (-0.5)
    for a in range(parts):
        rows = slice(a * part, (a + 1) * part)
        j = slot_ref[a]
        block = pre_ref[j, 0]
        cos, sin = cos_ref[rows], sin_ref[rows]
        q_s[rows] = turn(block[:, :HEAD], cos, sin).astype(BF)
        k_s[rows] = turn(block[:, HEAD : 2 * HEAD], cos, sin).astype(BF)
        v_s[rows] = block[:, 2 * HEAD :].astype(BF)
        g_s[rows] = gm_ref[j, 0]
    for first in range(0, L, SPAN):
        last = first + SPAN
        q, g = q_s[first:last], g_s[first:last]
        k, v = k_s[:last], v_s[:last]
        row = lax.broadcasted_iota(jnp.int32, (SPAN, 1), 0) + first
        limit = row
        for piece in range(2):
            low = starts_ref[2 * m + piece]
            limit = jnp.where((row >= low) & (row < low + PIECE), low + PIECE - 1, limit)
        column = lax.broadcasted_iota(jnp.int32, (SPAN, last), 1)
        scores = jnp.where(column <= limit, contract_last(q, k) * scale, -jnp.inf)
        top = jnp.max(scores, axis=1, keepdims=True)
        powers = jnp.exp(scores - top)
        probs = powers * (1.0 / jnp.sum(powers, axis=1, keepdims=True))
        pb = probs.astype(BF)
        mix = mm(pb, v).astype(BF)
        gp = contract_last(g, v)
        delta = jnp.sum(gp * probs, axis=1, keepdims=True)
        gs = (probs * (gp - delta)).astype(BF)
        gq = mm(gs, k) * scale
        gk = contract_first(gs, q)
        gv = contract_first(pb, g)
        if first == 0:
            gk_s[:last] = gk
            gv_s[:last] = gv
            gk_s[last:] = jnp.zeros((L - last, HEAD), F32)
            gv_s[last:] = jnp.zeros((L - last, HEAD), F32)
        else:
            gk_s[:last] += gk
            gv_s[:last] += gv
        for a in range(first // part, last // part):
            rows = slice(a * part - first, (a + 1) * part - first)
            table = slice(a * part, (a + 1) * part)
            j = slot_ref[a]
            mix_ref[j, 0] = mix[rows]
            grad_ref[j, 0, :, :HEAD] = turn(gq[rows], cos_ref[table], -sin_ref[table]).astype(BF)
    for a in range(parts):
        rows = slice(a * part, (a + 1) * part)
        j = slot_ref[a]
        gk = gk_s[rows] * scale
        grad_ref[j, 0, :, HEAD : 2 * HEAD] = turn(gk, cos_ref[rows], -sin_ref[rows]).astype(BF)
        grad_ref[j, 0, :, 2 * HEAD :] = gv_s[rows].astype(BF)


def attention(slots, starts, merged_pre, grad_mix, tables, micro, parts):
    part = L // parts
    heads = merged_pre.shape[1] // (3 * HEAD)
    cos, sin = tables
    pre = merged_pre.reshape(parts, micro, part, heads * 3 * HEAD)
    gm = grad_mix.reshape(parts, micro, part, heads * HEAD)
    spec = lambda w: pl.BlockSpec((parts, 1, part, w), lambda h, m, *_: (0, m, 0, h))
    table = pl.BlockSpec((L, 128), lambda h, m, *_: (0, 0))
    flops = heads * micro * 2 * 5 * L * L * HEAD * 3 // 4
    mix, grads = pl.pallas_call(
        functools.partial(attention_kernel, parts=parts, part=part),
        out_shape=(
            jax.ShapeDtypeStruct(gm.shape, BF),
            jax.ShapeDtypeStruct(pre.shape, BF),
        ),
        grid_spec=pltpu.PrefetchScalarGridSpec(
            num_scalar_prefetch=2,
            grid=(heads, micro),
            in_specs=[spec(3 * HEAD), spec(HEAD), table, table],
            out_specs=[spec(HEAD), spec(3 * HEAD)],
            scratch_shapes=[pltpu.VMEM((L, HEAD), BF)] * 4 + [pltpu.VMEM((L, HEAD), F32)] * 2,
        ),
        compiler_params=pltpu.CompilerParams(
            dimension_semantics=("arbitrary", "arbitrary"), vmem_limit_bytes=60 << 20
        ),
        cost_estimate=pl.CostEstimate(
            flops=2 * flops, bytes_accessed=pre.size * 6 + gm.size * 4, transcendentals=heads * micro * L * L
        ),
        name="attention",
    )(slots, starts, pre, gm, cos, sin)
    return mix.reshape(-1, heads * HEAD), grads.reshape(-1, heads * 3 * HEAD)


def after(value, *earlier):
    return lax.optimization_barrier((value,) + earlier)[0]


def ring_order(rows):
    if rows < 4:
        return list(range(rows))
    half = rows // 2
    return list(range(half)) + list(range(rows - 1, half - 1, -1))


def body(
    inputs,
    piece_starts,
    first_gain,
    first_shift,
    second_gain,
    second_shift,
    merged_weight,
    merged_bias,
    output_weight,
    output_bias,
    expand_weight,
    expand_bias,
    reduce_weight,
    reduce_bias,
    cotangent,
):
    rows = lax.axis_size("row")
    cols = lax.axis_size("col")
    micro, own_tokens, width = inputs.shape
    per_row = own_tokens // L
    part = L // rows
    block_rows = micro * part
    order = ring_order(rows)
    spot = [order.index(r) for r in range(rows)]
    ahead = [(order[i], order[(i + 1) % rows]) for i in range(rows)]
    behind = [(b, a) for a, b in ahead]
    me = lax.axis_index("row")
    my_spot = jnp.asarray(spot, jnp.int32)[me]
    slots = (jnp.asarray(spot, jnp.int32) - my_spot) % rows
    up = lambda v: lax.ppermute(v, "row", ahead)
    down = lambda v: lax.ppermute(v, "row", behind)

    def row_swap(own):
        b = own.reshape(micro, per_row, rows, part, width).transpose(2, 1, 0, 3, 4)
        b = lax.all_to_all(b, "row", split_axis=0, concat_axis=0, tiled=True)
        return b.reshape(rows * per_row, block_rows, width)

    def col_swap(b):
        return lax.all_to_all(b, "col", split_axis=0, concat_axis=0, tiled=True)

    def side_by_side(b):
        return b.transpose(1, 0, 2).reshape(block_rows, cols * width)

    def from_rows(block, *earlier):
        b = block.reshape(block_rows, cols, width).transpose(1, 0, 2)
        b = col_swap(b).reshape(rows, per_row, micro, part, width)
        if earlier:
            b = lax.all_to_all(after(b, *earlier), "row", split_axis=0, concat_axis=0, tiled=True)
            return b.transpose(2, 1, 0, 3, 4).reshape(micro, own_tokens, width)
        b = b.transpose(0, 2, 1, 3, 4)
        whole = jnp.zeros((micro, per_row, rows, part, width), BF)
        for step in range(rows):
            other = partner(me, step)
            source = me ^ step if rows & (rows - 1) == 0 else (me - step) % rows
            piece = lax.dynamic_index_in_dim(b, other, 0, keepdims=False)
            if step:
                piece = lax.ppermute(piece, "row", [(r, partner(r, step)) for r in range(rows)])
            whole = lax.dynamic_update_slice_in_dim(whole, piece[:, :, None], source, 2)
        return whole.reshape(micro, own_tokens, width)

    def partner(r, step):
        return r ^ step if rows & (rows - 1) == 0 else (r + step) % rows

    far = rows // 2
    cut = block_rows // 2

    def ring_gather(own, *earlier):
        pieces = [None] * rows
        pieces[0] = own
        fore, back = own, own
        for step in range(1, far):
            fore, back = up(fore), down(back)
            pieces[rows - step], pieces[step] = fore, back
        if earlier:
            fore, back = lax.optimization_barrier((fore, back) + earlier)[:2]
        pieces[far] = jnp.concatenate([up(fore[:cut]), down(back[cut:])], axis=0)
        return jnp.concatenate(pieces, axis=0)

    def chunk(total, j):
        return total[j * block_rows : (j + 1) * block_rows]

    def ring_open(total):
        last = chunk(total, far)
        return up(last[:cut]), down(last[cut:])

    def ring_close(total, halves):
        half_up, half_down = halves
        fore = back = None
        for step in range(far - 1, 0, -1):
            a, b = chunk(total, step).astype(F32), chunk(total, rows - step).astype(F32)
            if fore is None:
                a = jnp.concatenate([a[:cut] + half_up.astype(F32), a[cut:]], axis=0)
                b = jnp.concatenate([b[:cut], b[cut:] + half_down.astype(F32)], axis=0)
            else:
                a, b = a + fore.astype(F32), b + back.astype(F32)
            fore, back = up(a.astype(BF)), down(b.astype(BF))
        return chunk(total, 0).astype(F32) + fore.astype(F32) + back.astype(F32)

    def norm(block):
        block = block.astype(F32)
        center = jnp.mean(block, axis=-1, keepdims=True)
        spread = jnp.mean((block - center) ** 2, axis=-1, keepdims=True)
        inverse_std = lax.rsqrt(spread + norm_eps)
        return (block - center) * inverse_std, inverse_std

    def broadcast(value, axis, size):
        return lax.all_to_all(
            jnp.broadcast_to(value, (size,) + value.shape), axis, split_axis=0, concat_axis=0, tiled=True
        )

    gains = jnp.stack([first_gain, first_shift, second_gain, second_shift])
    spread_gains = broadcast(gains, "col", cols)
    gains = spread_gains.transpose(1, 0, 2).reshape(4, cols * width)
    expand_w = lax.all_gather(expand_weight, "col", axis=0, tiled=True)
    x_half = row_swap(after(inputs, spread_gains))
    cot_half = row_swap(after(cotangent, x_half))
    x_part = col_swap(after(x_half, cot_half))
    reduce_w = lax.all_gather(after(reduce_weight, x_part), "col", axis=1, tiled=True)
    mixed_weight = jnp.concatenate([merged_weight, output_weight.T], axis=1)
    cot_part = col_swap(after(cot_half, x_part))
    merged_cols = merged_weight.shape[1]
    x_part = side_by_side(x_part)
    x_seq = ring_gather(x_part)

    normed, _ = norm(x_seq)
    attend_in = (normed * gains[0] + gains[1]).astype(BF)
    expand_in = (normed * gains[2] + gains[3]).astype(BF)

    expand_pre = lax.optimization_barrier(mm(expand_in, expand_w) + expand_bias)
    cot_part = side_by_side(after(cot_part, expand_pre[:8, :128]))
    mixed_w = lax.all_gather(after(mixed_weight, cot_part), "col", axis=0, tiled=True)
    merged_w, output_wt = mixed_w[:, :merged_cols], mixed_w[:, merged_cols:]
    phi_sum = 0.5 * (1.0 + lax.erf(expand_pre * (0.5 ** 0.5)))
    density = jnp.exp(-0.5 * expand_pre * expand_pre) * 0.3989422804014327
    activated = (expand_pre * phi_sum).astype(BF)
    slope = (phi_sum + expand_pre * density).astype(BF)
    activated, slope = lax.optimization_barrier((activated, slope))
    branch_ff = mm(activated, reduce_w).astype(BF)
    cot_seq = ring_gather(cot_part, branch_ff)

    def scatter_weight(grad):
        return lax.psum_scatter(grad, "col", scatter_dimension=0, tiled=True).astype(F32)

    cot_seq, branch_ff, attend_in, *tables = lax.optimization_barrier(
        (cot_seq, branch_ff, attend_in) + rotary_tables()
    )
    reduce_dot = contract_first(cot_seq, activated).astype(BF)
    reduce_grad = scatter_weight(reduce_dot).T
    grad_act = contract_last(after(cot_seq, reduce_dot), reduce_w)
    grad_pre = (grad_act * slope.astype(F32)).astype(BF)
    expand_b = jnp.sum(grad_pre.astype(F32), axis=0)
    expand_dot = contract_first(expand_in, grad_pre).astype(BF)
    expand_grad = scatter_weight(expand_dot)

    merged_pre = mm(after(attend_in, expand_dot), merged_w) + merged_bias
    grad_mix = mm(after(cot_seq, expand_dot), output_wt).astype(BF)
    mix, grad_merged = attention(
        slots, piece_starts.reshape(-1), merged_pre, grad_mix, tables, micro, rows
    )
    branch = (contract_last(mix, output_wt) + branch_ff).astype(BF)
    halves = ring_open(branch)
    grad_merged, attend_late = lax.optimization_barrier(
        (grad_merged, attend_in, branch, reduce_grad)
    )[:2]
    merged_dot = contract_first(attend_late, grad_merged).astype(BF)
    merged_grad = scatter_weight(merged_dot)

    grad_merged, grad_pre, half_up, half_down = lax.optimization_barrier(
        (grad_merged, grad_pre) + halves + (merged_dot,)
    )[:4]
    branch = ring_close(branch, (half_up, half_down))
    grad_first = contract_last(grad_merged, merged_w)
    grad_second = contract_last(grad_pre, expand_w)
    norm_sums = jnp.stack(
        [
            jnp.sum(grad_first * normed, axis=0),
            jnp.sum(grad_first, axis=0),
            jnp.sum(grad_second * normed, axis=0),
            jnp.sum(grad_second, axis=0),
        ]
    )
    grad_hat = (grad_first * gains[0] + grad_second * gains[2]).astype(BF)
    halves = ring_open(grad_hat)
    merged_b = jnp.sum(grad_merged.astype(F32), axis=0)
    shift_b = jnp.sum(cotangent.astype(F32), axis=(0, 1))
    sums = jnp.concatenate(
        [
            norm_sums.reshape(4, cols, width).transpose(1, 0, 2).reshape(cols, 4 * width),
            jnp.broadcast_to(merged_b, (cols, merged_cols)),
            jnp.broadcast_to(expand_b, (cols, expand_b.shape[0])),
        ],
        axis=1,
    ).reshape(cols, -1, 128)
    spread_sums = lax.all_to_all(sums, "col", split_axis=0, concat_axis=0, tiled=True)
    mix_late, cot_late = lax.optimization_barrier(
        (mix, cot_seq, grad_hat, expand_grad, branch, spread_sums)
    )[:2]
    output_dot = contract_first(cot_late, mix_late).astype(BF)
    output_grad = scatter_weight(after(output_dot, merged_grad)).T
    halves = lax.optimization_barrier(halves + (output_dot,))[:2]
    grad_hat = ring_close(grad_hat, halves)
    sums = jnp.sum(spread_sums.reshape(cols, -1), axis=0)
    merged_b = sums[4 * width : 4 * width + merged_cols]
    expand_b = sums[4 * width + merged_cols :]
    tail = jnp.concatenate([sums[: 4 * width], shift_b]).reshape(-1, 128)
    if rows & (rows - 1) == 0:
        step = 1
        while step < rows:
            far_tail = lax.ppermute(tail, "row", [(r, r ^ step) for r in range(rows)])
            tail = tail + far_tail
            step *= 2
    else:
        far_tail = broadcast(tail, "row", rows)
        tail = jnp.sum(far_tail, axis=0)
    tail = tail.reshape(5, width)
    branch = from_rows(branch.astype(BF))
    result = inputs.astype(F32) + branch.astype(F32) + output_bias + reduce_bias
    result = result.astype(BF)

    part_normed, part_inverse = norm(x_part)
    norm_part = part_inverse * (
        grad_hat
        - jnp.mean(grad_hat, axis=-1, keepdims=True)
        - part_normed * jnp.mean(grad_hat * part_normed, axis=-1, keepdims=True)
    )

    norm_part = after(norm_part.astype(BF), output_grad, merged_grad)
    input_grad = cotangent.astype(F32) + from_rows(norm_part, result, far_tail).astype(F32)
    norm_sums, shift_b = tail[:4], tail[4]
    return (
        result,
        input_grad,
        norm_sums[0],
        norm_sums[1],
        norm_sums[2],
        norm_sums[3],
        merged_grad,
        merged_b,
        output_grad,
        shift_b,
        expand_grad,
        expand_b,
        reduce_grad,
        shift_b,
    )


def solution(mesh):
    in_specs = (
        P(None, "row", "col"),
        P(None, "col", None),
        P("col"),
        P("col"),
        P("col"),
        P("col"),
        P("col", "row"),
        P("row"),
        P("row", "col"),
        P("col"),
        P("col", "row"),
        P("row"),
        P("row", "col"),
        P("col"),
        P(None, "row", "col"),
    )
    out_specs = (
        P(None, "row", "col"),
        P(None, "row", "col"),
        P("col"),
        P("col"),
        P("col"),
        P("col"),
        P("col", "row"),
        P("row"),
        P("row", "col"),
        P("col"),
        P("col", "row"),
        P("row"),
        P("row", "col"),
        P("col"),
    )
    return jax.shard_map(body, mesh=mesh, in_specs=in_specs, out_specs=out_specs, check_vma=False)
```

```python
import functools

import jax
import jax.numpy as jnp
from jax import lax
from jax.experimental import pallas as pl
from jax.experimental.pallas import tpu as pltpu
from jax.sharding import PartitionSpec as P

D = 2048
HEAD = 256
ROT = 64
L = 1024
PIECE = 256
SPAN = 512

norm_eps = 1e-05
theta_base = 10000.0
BF = jnp.bfloat16
F32 = jnp.float32


def mm(left, right):
    return jnp.dot(left, right, preferred_element_type=F32)


def contract_last(left, right):
    return lax.dot_general(left, right, (((1,), (1,)), ((), ())), preferred_element_type=F32)


def contract_first(left, right):
    return lax.dot_general(left, right, (((0,), (0,)), ((), ())), preferred_element_type=F32)


def rotary_tables():
    half = ROT // 2
    freq_steps = jnp.arange(half, dtype=F32)
    inverse = jnp.power(theta_base, -(2.0 * freq_steps) / ROT)
    angles = jnp.arange(L, dtype=jnp.int32).astype(F32)[:, None] * inverse[None, :]
    cosine = jnp.cos(angles)
    sine = jnp.sin(angles)
    rest = 128 - ROT
    cos_table = jnp.concatenate([cosine, cosine, jnp.ones((L, rest), F32)], axis=1)
    sin_table = jnp.concatenate([-sine, sine, jnp.zeros((L, rest), F32)], axis=1)
    return cos_table, sin_table


def turn(block, cos, sin):
    half = ROT // 2
    head = block[:, :128]
    lane = lax.broadcasted_iota(jnp.int32, head.shape, 1)
    partner = jnp.where(lane < half, pltpu.roll(head, 128 - half, 1), pltpu.roll(head, half, 1))
    return jnp.concatenate([head * cos + partner * sin, block[:, 128:]], axis=1)


def attention_kernel(
    slot_ref, starts_ref, pre_ref, gm_ref, cos_ref, sin_ref,
    mix_ref, grad_ref, q_s, k_s, v_s, g_s, gk_s, gv_s, *, parts, part,
):
    m = pl.program_id(1)
    scale = HEAD ** (-0.5)
    for a in range(parts):
        rows = slice(a * part, (a + 1) * part)
        j = slot_ref[a]
        block = pre_ref[j, 0]
        cos, sin = cos_ref[rows], sin_ref[rows]
        q_s[rows] = turn(block[:, :HEAD], cos, sin).astype(BF)
        k_s[rows] = turn(block[:, HEAD : 2 * HEAD], cos, sin).astype(BF)
        v_s[rows] = block[:, 2 * HEAD :].astype(BF)
        g_s[rows] = gm_ref[j, 0]
    for first in range(0, L, SPAN):
        last = first + SPAN
        q, g = q_s[first:last], g_s[first:last]
        k, v = k_s[:last], v_s[:last]
        row = lax.broadcasted_iota(jnp.int32, (SPAN, 1), 0) + first
        limit = row
        for piece in range(2):
            low = starts_ref[2 * m + piece]
            limit = jnp.where((row >= low) & (row < low + PIECE), low + PIECE - 1, limit)
        column = lax.broadcasted_iota(jnp.int32, (SPAN, last), 1)
        scores = jnp.where(column <= limit, contract_last(q, k) * scale, -jnp.inf)
        top = jnp.max(scores, axis=1, keepdims=True)
        powers = jnp.exp(scores - top)
        probs = powers * (1.0 / jnp.sum(powers, axis=1, keepdims=True))
        pb = probs.astype(BF)
        mix = mm(pb, v).astype(BF)
        gp = contract_last(g, v)
        delta = jnp.sum(gp * probs, axis=1, keepdims=True)
        gs = (probs * (gp - delta)).astype(BF)
        gq = mm(gs, k) * scale
        gk = contract_first(gs, q)
        gv = contract_first(pb, g)
        if first == 0:
            gk_s[:last] = gk
            gv_s[:last] = gv
            gk_s[last:] = jnp.zeros((L - last, HEAD), F32)
            gv_s[last:] = jnp.zeros((L - last, HEAD), F32)
        else:
            gk_s[:last] += gk
            gv_s[:last] += gv
        for a in range(first // part, last // part):
            rows = slice(a * part - first, (a + 1) * part - first)
            table = slice(a * part, (a + 1) * part)
            j = slot_ref[a]
            mix_ref[j, 0] = mix[rows]
            grad_ref[j, 0, :, :HEAD] = turn(gq[rows], cos_ref[table], -sin_ref[table]).astype(BF)
    for a in range(parts):
        rows = slice(a * part, (a + 1) * part)
        j = slot_ref[a]
        gk = gk_s[rows] * scale
        grad_ref[j, 0, :, HEAD : 2 * HEAD] = turn(gk, cos_ref[rows], -sin_ref[rows]).astype(BF)
        grad_ref[j, 0, :, 2 * HEAD :] = gv_s[rows].astype(BF)


def attention(slots, starts, merged_pre, grad_mix, tables, micro, parts):
    part = L // parts
    heads = merged_pre.shape[1] // (3 * HEAD)
    cos, sin = tables
    pre = merged_pre.reshape(parts, micro, part, heads * 3 * HEAD)
    gm = grad_mix.reshape(parts, micro, part, heads * HEAD)
    spec = lambda w: pl.BlockSpec((parts, 1, part, w), lambda h, m, *_: (0, m, 0, h))
    table = pl.BlockSpec((L, 128), lambda h, m, *_: (0, 0))
    flops = heads * micro * 2 * 5 * L * L * HEAD * 3 // 4
    mix, grads = pl.pallas_call(
        functools.partial(attention_kernel, parts=parts, part=part),
        out_shape=(
            jax.ShapeDtypeStruct(gm.shape, BF),
            jax.ShapeDtypeStruct(pre.shape, BF),
        ),
        grid_spec=pltpu.PrefetchScalarGridSpec(
            num_scalar_prefetch=2,
            grid=(heads, micro),
            in_specs=[spec(3 * HEAD), spec(HEAD), table, table],
            out_specs=[spec(HEAD), spec(3 * HEAD)],
            scratch_shapes=[pltpu.VMEM((L, HEAD), BF)] * 4 + [pltpu.VMEM((L, HEAD), F32)] * 2,
        ),
        compiler_params=pltpu.CompilerParams(
            dimension_semantics=("arbitrary", "arbitrary"), vmem_limit_bytes=60 << 20
        ),
        cost_estimate=pl.CostEstimate(
            flops=2 * flops, bytes_accessed=pre.size * 6 + gm.size * 4, transcendentals=heads * micro * L * L
        ),
        name="attention",
    )(slots, starts, pre, gm, cos, sin)
    return mix.reshape(-1, heads * HEAD), grads.reshape(-1, heads * 3 * HEAD)


def after(value, *earlier):
    return lax.optimization_barrier((value,) + earlier)[0]


def ring_order(rows):
    if rows < 4:
        return list(range(rows))
    half = rows // 2
    return list(range(half)) + list(range(rows - 1, half - 1, -1))


def body(
    inputs,
    piece_starts,
    first_gain,
    first_shift,
    second_gain,
    second_shift,
    merged_weight,
    merged_bias,
    output_weight,
    output_bias,
    expand_weight,
    expand_bias,
    reduce_weight,
    reduce_bias,
    cotangent,
):
    rows = lax.axis_size("row")
    cols = lax.axis_size("col")
    micro, own_tokens, width = inputs.shape
    per_row = own_tokens // L
    part = L // rows
    block_rows = micro * part
    order = ring_order(rows)
    spot = [order.index(r) for r in range(rows)]
    ahead = [(order[i], order[(i + 1) % rows]) for i in range(rows)]
    behind = [(b, a) for a, b in ahead]
    me = lax.axis_index("row")
    my_spot = jnp.asarray(spot, jnp.int32)[me]
    slots = (jnp.asarray(spot, jnp.int32) - my_spot) % rows
    up = lambda v: lax.ppermute(v, "row", ahead)
    down = lambda v: lax.ppermute(v, "row", behind)

    def row_swap(own):
        b = own.reshape(micro, per_row, rows, part, width).transpose(2, 1, 0, 3, 4)
        b = lax.all_to_all(b, "row", split_axis=0, concat_axis=0, tiled=True)
        return b.reshape(rows * per_row, block_rows, width)

    def col_swap(b):
        return lax.all_to_all(b, "col", split_axis=0, concat_axis=0, tiled=True)

    def side_by_side(b):
        return b.transpose(1, 0, 2).reshape(block_rows, cols * width)

    def from_rows(block, *earlier):
        b = block.reshape(block_rows, cols, width).transpose(1, 0, 2)
        b = col_swap(b).reshape(rows, per_row, micro, part, width)
        if earlier:
            b = lax.all_to_all(after(b, *earlier), "row", split_axis=0, concat_axis=0, tiled=True)
            return b.transpose(2, 1, 0, 3, 4).reshape(micro, own_tokens, width)
        b = b.transpose(0, 2, 1, 3, 4)
        whole = jnp.zeros((micro, per_row, rows, part, width), BF)
        for step in range(rows):
            other = partner(me, step)
            source = me ^ step if rows & (rows - 1) == 0 else (me - step) % rows
            piece = lax.dynamic_index_in_dim(b, other, 0, keepdims=False)
            if step:
                piece = lax.ppermute(piece, "row", [(r, partner(r, step)) for r in range(rows)])
            whole = lax.dynamic_update_slice_in_dim(whole, piece[:, :, None], source, 2)
        return whole.reshape(micro, own_tokens, width)

    def partner(r, step):
        return r ^ step if rows & (rows - 1) == 0 else (r + step) % rows

    far = rows // 2
    cut = block_rows // 2

    def ring_gather(own, *earlier):
        pieces = [None] * rows
        pieces[0] = own
        fore, back = own, own
        for step in range(1, far):
            fore, back = up(fore), down(back)
            pieces[rows - step], pieces[step] = fore, back
        if earlier:
            fore, back = lax.optimization_barrier((fore, back) + earlier)[:2]
        pieces[far] = jnp.concatenate([up(fore[:cut]), down(back[cut:])], axis=0)
        return pieces

    def chunk(total, j):
        return total[j * block_rows : (j + 1) * block_rows]

    def ring_open(total):
        last = chunk(total, far)
        return up(last[:cut]), down(last[cut:])

    def ring_close(total, halves):
        half_up, half_down = halves
        fore = back = None
        for step in range(far - 1, 0, -1):
            a, b = chunk(total, step).astype(F32), chunk(total, rows - step).astype(F32)
            if fore is None:
                a = jnp.concatenate([a[:cut] + half_up.astype(F32), a[cut:]], axis=0)
                b = jnp.concatenate([b[:cut], b[cut:] + half_down.astype(F32)], axis=0)
            else:
                a, b = a + fore.astype(F32), b + back.astype(F32)
            fore, back = up(a.astype(BF)), down(b.astype(BF))
        return chunk(total, 0).astype(F32) + fore.astype(F32) + back.astype(F32)

    def norm(block):
        block = block.astype(F32)
        center = jnp.mean(block, axis=-1, keepdims=True)
        spread = jnp.mean((block - center) ** 2, axis=-1, keepdims=True)
        inverse_std = lax.rsqrt(spread + norm_eps)
        return (block - center) * inverse_std, inverse_std

    def broadcast(value, axis, size):
        return lax.all_to_all(
            jnp.broadcast_to(value, (size,) + value.shape), axis, split_axis=0, concat_axis=0, tiled=True
        )

    gains = jnp.stack([first_gain, first_shift, second_gain, second_shift])
    def add_up(value, axis, size):
        if size & (size - 1):
            spread = broadcast(value, axis, size)
            return jnp.sum(spread, axis=0), spread
        step = 1
        while step < size:
            taken = lax.ppermute(value, axis, [(r, r ^ step) for r in range(size)])
            value = value + taken
            step *= 2
        return value, taken

    spread_gains = broadcast(gains, "col", cols)
    gains = spread_gains.transpose(1, 0, 2).reshape(4, cols * width)
    expand_w = lax.all_gather(expand_weight, "col", axis=0, tiled=True)
    x_half = row_swap(after(inputs, spread_gains))
    cot_half = row_swap(after(cotangent, x_half))
    x_part = col_swap(after(x_half, cot_half))
    cot_part = col_swap(after(cot_half, x_part))
    x_part = side_by_side(x_part)
    x_pieces = ring_gather(x_part)
    x_seq = jnp.concatenate(x_pieces, axis=0)
    reduce_weight = after(reduce_weight, x_pieces[1], x_pieces[-1], cot_part)
    reduce_w = lax.all_gather(reduce_weight, "col", axis=1, tiled=True)
    merged_cols = merged_weight.shape[1]
    mixed_weight = jnp.concatenate([merged_weight, output_weight.T], axis=1)
    mixed_w = lax.all_gather(after(mixed_weight, cot_part), "col", axis=0, tiled=True)
    merged_w, output_wt = mixed_w[:, :merged_cols], mixed_w[:, merged_cols:]

    normed, _ = norm(x_seq)
    attend_in = (normed * gains[0] + gains[1]).astype(BF)
    expand_in = (normed * gains[2] + gains[3]).astype(BF)

    expand_pre = lax.optimization_barrier(mm(expand_in, expand_w) + expand_bias)
    cot_part = side_by_side(after(cot_part, x_seq))
    phi_sum = 0.5 * (1.0 + lax.erf(expand_pre * (0.5 ** 0.5)))
    density = jnp.exp(-0.5 * expand_pre * expand_pre) * 0.3989422804014327
    activated = (expand_pre * phi_sum).astype(BF)
    slope = (phi_sum + expand_pre * density).astype(BF)
    activated, slope = lax.optimization_barrier((activated, slope))
    core = lax.axis_index("col") % 2
    other_core = [(c, c ^ 1) for c in range(cols)]
    chips = [list(range(k, cols, 2)) for k in range(2)]

    def own_and_other(value):
        blocks = [value[:, c * width : (c + 1) * width] for c in range(cols)]
        even, odd = blocks[::2], blocks[1::2]
        own = [jnp.where(core == 0, a, b) for a, b in zip(even, odd)]
        other = [jnp.where(core == 0, b, a) for a, b in zip(even, odd)]
        return jnp.concatenate(own, axis=1), jnp.concatenate(other, axis=1)

    cot_pieces = ring_gather(cot_part, activated)
    cot_seq = jnp.concatenate(cot_pieces, axis=0)
    cot_own, cot_other = (
        jnp.concatenate(part, axis=0) for part in zip(*[own_and_other(p) for p in cot_pieces])
    )
    ready = (attend_in,) + own_and_other(expand_in) + own_and_other(attend_in) + rotary_tables()
    cot_other, attend_in, expand_own, expand_other, attend_own, attend_other, *tables = (
        lax.optimization_barrier((cot_other,) + ready)
    )

    def give(other, grad):
        sent = contract_first(other, grad).astype(BF)
        return sent, lax.ppermute(sent, "col", other_core)

    def keep(own, grad, taken):
        return (contract_first(own, grad) + taken.astype(F32)).astype(BF)

    def scatter_weight(grad):
        grad = lax.psum_scatter(
            grad, "col", scatter_dimension=0, tiled=True, axis_index_groups=chips
        )
        return grad.astype(F32)

    reduce_sent, reduce_taken = give(cot_other, activated)
    branch_ff = mm(after(activated, reduce_sent), reduce_w).astype(BF)
    reduce_dot = keep(after(cot_own, branch_ff), activated, reduce_taken)
    reduce_grad = scatter_weight(reduce_dot).T
    grad_act = contract_last(after(cot_seq, reduce_dot), reduce_w)
    grad_pre = (grad_act * slope.astype(F32)).astype(BF)
    expand_b = jnp.sum(grad_pre.astype(F32), axis=0)
    expand_sent, expand_taken = give(expand_other, grad_pre)
    grad_mix = mm(after(cot_seq, expand_sent), output_wt).astype(BF)
    merged_pre = mm(after(attend_in, grad_mix), merged_w) + merged_bias
    mix, grad_merged = attention(
        slots, piece_starts.reshape(-1), merged_pre, grad_mix, tables, micro, rows
    )
    mix = after(mix, reduce_grad)
    branch = (contract_last(mix, output_wt) + branch_ff).astype(BF)
    halves = ring_open(branch)
    expand_dot = keep(after(expand_own, branch), grad_pre, expand_taken)
    expand_grad = scatter_weight(expand_dot)
    grad_merged, attend_other = lax.optimization_barrier(
        (grad_merged, attend_other, branch)
    )[:2]
    merged_sent, merged_taken = give(attend_other, grad_merged)
    grad_merged, grad_pre, half_up, half_down = lax.optimization_barrier(
        (grad_merged, grad_pre) + halves + (merged_sent,)
    )[:4]
    merged_dot = keep(attend_own, grad_merged, merged_taken)
    merged_grad = scatter_weight(merged_dot)
    branch = ring_close(branch, (half_up, half_down))
    grad_first = contract_last(grad_merged, merged_w)
    grad_second = contract_last(grad_pre, expand_w)
    norm_sums = jnp.stack(
        [
            jnp.sum(grad_first * normed, axis=0),
            jnp.sum(grad_first, axis=0),
            jnp.sum(grad_second * normed, axis=0),
            jnp.sum(grad_second, axis=0),
        ]
    )
    grad_hat = (grad_first * gains[0] + grad_second * gains[2]).astype(BF)
    halves = ring_open(grad_hat)
    merged_b = jnp.sum(grad_merged.astype(F32), axis=0)
    shift_b = jnp.sum(cotangent.astype(F32), axis=(0, 1))
    sums, far_sums = add_up(
        jnp.concatenate([norm_sums.reshape(-1), merged_b, expand_b]).reshape(-1, 128), "col", cols
    )
    mix = lax.optimization_barrier((mix, grad_hat, expand_grad, branch, merged_dot))[0]
    output_sent, output_taken = give(cot_other, mix)
    output_dot = keep(cot_own, mix, output_taken)
    output_grad = scatter_weight(after(output_dot, merged_grad)).T
    halves = lax.optimization_barrier(halves + (output_sent,))[:2]
    grad_hat = ring_close(grad_hat, halves)
    own_sums = lax.dynamic_index_in_dim(
        sums[: 4 * cols * width // 128].reshape(4, cols, -1, 128), lax.axis_index("col"), 1, keepdims=False
    )
    biases = sums[4 * cols * width // 128 :].reshape(-1)
    merged_b, expand_b = biases[:merged_cols], biases[merged_cols:]
    tail, far_tail = add_up(
        jnp.concatenate([own_sums.reshape(-1, 128), shift_b.reshape(-1, 128)]), "row", rows
    )
    tail = tail.reshape(5, width)
    branch = from_rows(branch.astype(BF))
    result = inputs.astype(F32) + branch.astype(F32) + output_bias + reduce_bias
    result = result.astype(BF)

    part_normed, part_inverse = norm(x_part)
    norm_part = part_inverse * (
        grad_hat
        - jnp.mean(grad_hat, axis=-1, keepdims=True)
        - part_normed * jnp.mean(grad_hat * part_normed, axis=-1, keepdims=True)
    )

    norm_part = after(norm_part.astype(BF), output_grad, merged_grad)
    input_grad = cotangent.astype(F32) + from_rows(norm_part, result, far_tail).astype(F32)
    norm_sums, shift_b = tail[:4], tail[4]
    return (
        result,
        input_grad,
        norm_sums[0],
        norm_sums[1],
        norm_sums[2],
        norm_sums[3],
        merged_grad,
        merged_b,
        output_grad,
        shift_b,
        expand_grad,
        expand_b,
        reduce_grad,
        shift_b,
    )


def solution(mesh):
    in_specs = (
        P(None, "row", "col"),
        P(None, "col", None),
        P("col"),
        P("col"),
        P("col"),
        P("col"),
        P("col", "row"),
        P("row"),
        P("row", "col"),
        P("col"),
        P("col", "row"),
        P("row"),
        P("row", "col"),
        P("col"),
        P(None, "row", "col"),
    )
    out_specs = (
        P(None, "row", "col"),
        P(None, "row", "col"),
        P("col"),
        P("col"),
        P("col"),
        P("col"),
        P("col", "row"),
        P("row"),
        P("row", "col"),
        P("col"),
        P("col", "row"),
        P("row"),
        P("row", "col"),
        P("col"),
    )
    return jax.shard_map(body, mesh=mesh, in_specs=in_specs, out_specs=out_specs, check_vma=False)
```

```python
import functools

import jax
import jax.numpy as jnp
from jax import lax
from jax.experimental import pallas as pl
from jax.experimental.pallas import tpu as pltpu
from jax.sharding import PartitionSpec as P

D = 2048
HEAD = 256
ROT = 64
L = 1024
PIECE = 256
SPAN = 512

norm_eps = 1e-05
theta_base = 10000.0
BF = jnp.bfloat16
F32 = jnp.float32


def mm(left, right):
    return jnp.dot(left, right, preferred_element_type=F32)


def contract_last(left, right):
    return lax.dot_general(left, right, (((1,), (1,)), ((), ())), preferred_element_type=F32)


def contract_first(left, right):
    return lax.dot_general(left, right, (((0,), (0,)), ((), ())), preferred_element_type=F32)


def rotary_tables():
    half = ROT // 2
    freq_steps = jnp.arange(half, dtype=F32)
    inverse = jnp.power(theta_base, -(2.0 * freq_steps) / ROT)
    angles = jnp.arange(L, dtype=jnp.int32).astype(F32)[:, None] * inverse[None, :]
    cosine = jnp.cos(angles)
    sine = jnp.sin(angles)
    rest = 128 - ROT
    cos_table = jnp.concatenate([cosine, cosine, jnp.ones((L, rest), F32)], axis=1)
    sin_table = jnp.concatenate([-sine, sine, jnp.zeros((L, rest), F32)], axis=1)
    return cos_table, sin_table


def turn(block, cos, sin):
    half = ROT // 2
    head = block[:, :128]
    lane = lax.broadcasted_iota(jnp.int32, head.shape, 1)
    partner = jnp.where(lane < half, pltpu.roll(head, 128 - half, 1), pltpu.roll(head, half, 1))
    return jnp.concatenate([head * cos + partner * sin, block[:, 128:]], axis=1)


def attention_kernel(
    slot_ref, starts_ref, pre_ref, gm_ref, cos_ref, sin_ref,
    mix_ref, grad_ref, q_s, k_s, v_s, g_s, gk_s, gv_s, *, parts, part,
):
    m = pl.program_id(1)
    scale = HEAD ** (-0.5)
    for a in range(parts):
        rows = slice(a * part, (a + 1) * part)
        j = slot_ref[a]
        block = pre_ref[j, 0]
        cos, sin = cos_ref[rows], sin_ref[rows]
        q_s[rows] = turn(block[:, :HEAD], cos, sin).astype(BF)
        k_s[rows] = turn(block[:, HEAD : 2 * HEAD], cos, sin).astype(BF)
        v_s[rows] = block[:, 2 * HEAD :].astype(BF)
        g_s[rows] = gm_ref[j, 0]
    for first in range(0, L, SPAN):
        last = first + SPAN
        q, g = q_s[first:last], g_s[first:last]
        k, v = k_s[:last], v_s[:last]
        row = lax.broadcasted_iota(jnp.int32, (SPAN, 1), 0) + first
        limit = row
        for piece in range(2):
            low = starts_ref[2 * m + piece]
            limit = jnp.where((row >= low) & (row < low + PIECE), low + PIECE - 1, limit)
        column = lax.broadcasted_iota(jnp.int32, (SPAN, last), 1)
        scores = jnp.where(column <= limit, contract_last(q, k) * scale, -jnp.inf)
        top = jnp.max(scores, axis=1, keepdims=True)
        powers = jnp.exp(scores - top)
        probs = powers * (1.0 / jnp.sum(powers, axis=1, keepdims=True))
        pb = probs.astype(BF)
        mix = mm(pb, v).astype(BF)
        gp = contract_last(g, v)
        delta = jnp.sum(gp * probs, axis=1, keepdims=True)
        gs = (probs * (gp - delta)).astype(BF)
        gq = mm(gs, k) * scale
        gk = contract_first(gs, q)
        gv = contract_first(pb, g)
        if first == 0:
            gk_s[:last] = gk
            gv_s[:last] = gv
            gk_s[last:] = jnp.zeros((L - last, HEAD), F32)
            gv_s[last:] = jnp.zeros((L - last, HEAD), F32)
        else:
            gk_s[:last] += gk
            gv_s[:last] += gv
        for a in range(first // part, last // part):
            rows = slice(a * part - first, (a + 1) * part - first)
            table = slice(a * part, (a + 1) * part)
            j = slot_ref[a]
            mix_ref[j, 0] = mix[rows]
            grad_ref[j, 0, :, :HEAD] = turn(gq[rows], cos_ref[table], -sin_ref[table]).astype(BF)
    for a in range(parts):
        rows = slice(a * part, (a + 1) * part)
        j = slot_ref[a]
        gk = gk_s[rows] * scale
        grad_ref[j, 0, :, HEAD : 2 * HEAD] = turn(gk, cos_ref[rows], -sin_ref[rows]).astype(BF)
        grad_ref[j, 0, :, 2 * HEAD :] = gv_s[rows].astype(BF)


def attention(slots, starts, merged_pre, grad_mix, tables, micro, parts):
    part = L // parts
    heads = merged_pre.shape[1] // (3 * HEAD)
    cos, sin = tables
    pre = merged_pre.reshape(parts, micro, part, heads * 3 * HEAD)
    gm = grad_mix.reshape(parts, micro, part, heads * HEAD)
    spec = lambda w: pl.BlockSpec((parts, 1, part, w), lambda h, m, *_: (0, m, 0, h))
    table = pl.BlockSpec((L, 128), lambda h, m, *_: (0, 0))
    flops = heads * micro * 2 * 5 * L * L * HEAD * 3 // 4
    mix, grads = pl.pallas_call(
        functools.partial(attention_kernel, parts=parts, part=part),
        out_shape=(
            jax.ShapeDtypeStruct(gm.shape, BF),
            jax.ShapeDtypeStruct(pre.shape, BF),
        ),
        grid_spec=pltpu.PrefetchScalarGridSpec(
            num_scalar_prefetch=2,
            grid=(heads, micro),
            in_specs=[spec(3 * HEAD), spec(HEAD), table, table],
            out_specs=[spec(HEAD), spec(3 * HEAD)],
            scratch_shapes=[pltpu.VMEM((L, HEAD), BF)] * 4 + [pltpu.VMEM((L, HEAD), F32)] * 2,
        ),
        compiler_params=pltpu.CompilerParams(
            dimension_semantics=("arbitrary", "arbitrary"), vmem_limit_bytes=60 << 20
        ),
        cost_estimate=pl.CostEstimate(
            flops=2 * flops, bytes_accessed=pre.size * 6 + gm.size * 4, transcendentals=heads * micro * L * L
        ),
        name="attention",
    )(slots, starts, pre, gm, cos, sin)
    return mix.reshape(-1, heads * HEAD), grads.reshape(-1, heads * 3 * HEAD)


def after(value, *earlier):
    return lax.optimization_barrier((value,) + earlier)[0]


def ring_order(rows):
    if rows < 4:
        return list(range(rows))
    half = rows // 2
    return list(range(half)) + list(range(rows - 1, half - 1, -1))


def body(
    inputs,
    piece_starts,
    first_gain,
    first_shift,
    second_gain,
    second_shift,
    merged_weight,
    merged_bias,
    output_weight,
    output_bias,
    expand_weight,
    expand_bias,
    reduce_weight,
    reduce_bias,
    cotangent,
):
    rows = lax.axis_size("row")
    cols = lax.axis_size("col")
    micro, own_tokens, width = inputs.shape
    per_row = own_tokens // L
    part = L // rows
    block_rows = micro * part
    order = ring_order(rows)
    spot = [order.index(r) for r in range(rows)]
    ahead = [(order[i], order[(i + 1) % rows]) for i in range(rows)]
    behind = [(b, a) for a, b in ahead]
    me = lax.axis_index("row")
    my_spot = jnp.asarray(spot, jnp.int32)[me]
    slots = (jnp.asarray(spot, jnp.int32) - my_spot) % rows
    up = lambda v: lax.ppermute(v, "row", ahead)
    down = lambda v: lax.ppermute(v, "row", behind)

    def row_swap(own):
        b = own.reshape(micro, per_row, rows, part, width).transpose(2, 1, 0, 3, 4)
        b = lax.all_to_all(b, "row", split_axis=0, concat_axis=0, tiled=True)
        return b.reshape(rows * per_row, block_rows, width)

    def col_swap(b):
        return lax.all_to_all(b, "col", split_axis=0, concat_axis=0, tiled=True)

    def side_by_side(b):
        return b.transpose(1, 0, 2).reshape(block_rows, cols * width)

    def from_rows(block, *earlier):
        b = block.reshape(rows, per_row, micro, part, width)
        if earlier:
            b = lax.all_to_all(after(b, *earlier), "row", split_axis=0, concat_axis=0, tiled=True)
            return b.transpose(2, 1, 0, 3, 4).reshape(micro, own_tokens, width)
        b = b.transpose(0, 2, 1, 3, 4)
        whole = jnp.zeros((micro, per_row, rows, part, width), BF)
        for step in range(rows):
            other = partner(me, step)
            source = me ^ step if rows & (rows - 1) == 0 else (me - step) % rows
            piece = lax.dynamic_index_in_dim(b, other, 0, keepdims=False)
            if step:
                piece = lax.ppermute(piece, "row", [(r, partner(r, step)) for r in range(rows)])
            whole = lax.dynamic_update_slice_in_dim(whole, piece[:, :, None], source, 2)
        return whole.reshape(micro, own_tokens, width)

    def partner(r, step):
        return r ^ step if rows & (rows - 1) == 0 else (r + step) % rows

    far = rows // 2
    cut = block_rows // 2

    def ring_gather(own, *earlier):
        pieces = [None] * rows
        pieces[0] = own
        fore, back = own, own
        for step in range(1, far):
            fore, back = up(fore), down(back)
            pieces[rows - step], pieces[step] = fore, back
        if earlier:
            fore, back = lax.optimization_barrier((fore, back) + earlier)[:2]
        pieces[far] = jnp.concatenate([up(fore[:cut]), down(back[cut:])], axis=0)
        return pieces

    def chunk(total, j):
        return total[j * block_rows : (j + 1) * block_rows]

    def ring_open(total):
        last = chunk(total, far)
        return up(last[:cut]), down(last[cut:])

    def ring_close(total, halves):
        half_up, half_down = halves
        fore = back = None
        for step in range(far - 1, 0, -1):
            a, b = chunk(total, step).astype(F32), chunk(total, rows - step).astype(F32)
            if fore is None:
                a = jnp.concatenate([a[:cut] + half_up.astype(F32), a[cut:]], axis=0)
                b = jnp.concatenate([b[:cut], b[cut:] + half_down.astype(F32)], axis=0)
            else:
                a, b = a + fore.astype(F32), b + back.astype(F32)
            fore, back = up(a.astype(BF)), down(b.astype(BF))
        return chunk(total, 0), fore, back

    def norm(block):
        block = block.astype(F32)
        center = jnp.mean(block, axis=-1, keepdims=True)
        spread = jnp.mean((block - center) ** 2, axis=-1, keepdims=True)
        inverse_std = lax.rsqrt(spread + norm_eps)
        return (block - center) * inverse_std, inverse_std

    def broadcast(value, axis, size):
        return lax.all_to_all(
            jnp.broadcast_to(value, (size,) + value.shape), axis, split_axis=0, concat_axis=0, tiled=True
        )

    gains = jnp.stack([first_gain, first_shift, second_gain, second_shift])
    def add_up(value, axis, size):
        if size & (size - 1):
            spread = broadcast(value, axis, size)
            return jnp.sum(spread, axis=0), spread
        step = 1
        while step < size:
            taken = lax.ppermute(value, axis, [(r, r ^ step) for r in range(size)])
            value = value + taken
            step *= 2
        return value, taken

    spread_gains = broadcast(gains, "col", cols)
    gains = spread_gains.transpose(1, 0, 2).reshape(4, cols * width)
    expand_w = lax.all_gather(expand_weight, "col", axis=0, tiled=True)
    x_half = row_swap(after(inputs, spread_gains))
    cot_half = row_swap(after(cotangent, x_half))
    x_part = col_swap(after(x_half, cot_half))
    cot_part = col_swap(after(cot_half, x_part))
    x_part = side_by_side(x_part)
    x_pieces = ring_gather(x_part)
    x_seq = jnp.concatenate(x_pieces, axis=0)
    reduce_weight = after(reduce_weight, x_pieces[1], x_pieces[-1], cot_part)
    reduce_w = lax.all_gather(reduce_weight, "col", axis=1, tiled=True)
    merged_cols = merged_weight.shape[1]
    mixed_weight = jnp.concatenate([merged_weight, output_weight.T], axis=1)
    mixed_w = lax.all_gather(after(mixed_weight, cot_part), "col", axis=0, tiled=True)
    merged_w, output_wt = mixed_w[:, :merged_cols], mixed_w[:, merged_cols:]

    normed, _ = norm(x_seq)
    attend_in = (normed * gains[0] + gains[1]).astype(BF)
    expand_in = (normed * gains[2] + gains[3]).astype(BF)

    expand_pre = lax.optimization_barrier(mm(expand_in, expand_w) + expand_bias)
    cot_part = side_by_side(after(cot_part, x_seq))
    phi_sum = 0.5 * (1.0 + lax.erf(expand_pre * (0.5 ** 0.5)))
    density = jnp.exp(-0.5 * expand_pre * expand_pre) * 0.3989422804014327
    activated = (expand_pre * phi_sum).astype(BF)
    slope = (phi_sum + expand_pre * density).astype(BF)
    activated, slope = lax.optimization_barrier((activated, slope))
    core = lax.axis_index("col") % 2
    other_core = [(c, c ^ 1) for c in range(cols)]
    chips = [list(range(k, cols, 2)) for k in range(2)]

    def own_and_other(value):
        blocks = [value[:, c * width : (c + 1) * width] for c in range(cols)]
        even, odd = blocks[::2], blocks[1::2]
        own = [jnp.where(core == 0, a, b) for a, b in zip(even, odd)]
        other = [jnp.where(core == 0, b, a) for a, b in zip(even, odd)]
        return jnp.concatenate(own, axis=1), jnp.concatenate(other, axis=1)

    branch_ff = mm(activated, reduce_w).astype(BF)
    cot_seq = jnp.concatenate(ring_gather(cot_part, branch_ff), axis=0)
    cot_own, cot_other = own_and_other(cot_seq)
    ready = (attend_in,) + own_and_other(expand_in) + own_and_other(attend_in) + rotary_tables()
    cot_other, attend_in, expand_own, expand_other, attend_own, attend_other, *tables = (
        lax.optimization_barrier((cot_other,) + ready)
    )

    def give(other, grad):
        sent = contract_first(other, grad).astype(BF)
        return sent, lax.ppermute(sent, "col", other_core)

    def keep(own, grad, taken):
        return (contract_first(own, grad) + taken.astype(F32)).astype(BF)

    def scatter_weight(grad):
        grad = lax.psum_scatter(
            grad, "col", scatter_dimension=0, tiled=True, axis_index_groups=chips
        )
        return grad.astype(F32)

    reduce_sent, reduce_taken = give(cot_other, activated)
    reduce_dot = keep(after(cot_own, reduce_sent), activated, reduce_taken)
    reduce_grad = scatter_weight(reduce_dot).T
    grad_act = contract_last(after(cot_seq, reduce_dot, mixed_w), reduce_w)
    grad_pre = (grad_act * slope.astype(F32)).astype(BF)
    expand_b = jnp.sum(grad_pre.astype(F32), axis=0)
    expand_sent, expand_taken = give(expand_other, grad_pre)
    grad_mix = mm(after(cot_seq, expand_sent), output_wt).astype(BF)
    expand_dot = keep(after(expand_own, grad_mix), grad_pre, expand_taken)
    expand_grad = scatter_weight(expand_dot)
    merged_pre = mm(after(attend_in, expand_dot), merged_w) + merged_bias
    grad_mix = after(grad_mix, reduce_grad)
    mix, grad_merged = attention(
        slots, piece_starts.reshape(-1), merged_pre, grad_mix, tables, micro, rows
    )
    branch = (contract_last(mix, output_wt) + branch_ff).astype(BF)
    halves = ring_open(branch)
    grad_merged, attend_other = lax.optimization_barrier(
        (grad_merged, attend_other, branch)
    )[:2]
    merged_sent, merged_taken = give(attend_other, grad_merged)
    grad_merged, grad_pre, half_up, half_down = lax.optimization_barrier(
        (grad_merged, grad_pre) + halves + (merged_sent,)
    )[:4]
    branch_parts = ring_close(branch, (half_up, half_down))
    merged_dot = keep(attend_own, grad_merged, merged_taken)
    merged_grad = scatter_weight(merged_dot)
    grad_merged, grad_pre = lax.optimization_barrier(
        (grad_merged, grad_pre, merged_dot, expand_grad)
    )[:2]

    def grads(j, *earlier):
        first = contract_last(after(chunk(grad_merged, j), *earlier), merged_w)
        second = contract_last(after(chunk(grad_pre, j), *earlier), expand_w)
        normal = chunk(normed, j)
        sums = (
            jnp.sum(first * normal, axis=0),
            jnp.sum(first, axis=0),
            jnp.sum(second * normal, axis=0),
            jnp.sum(second, axis=0),
        )
        hat = (first * gains[0] + second * gains[2]).astype(BF)
        return lax.optimization_barrier((hat, sums))

    hat, sums = grads(far)
    chunk_sums = [sums]
    wide = lambda v: v.astype(F32)
    branch_parts = lax.optimization_barrier(branch_parts + (hat,))[:3]
    branch = wide(branch_parts[0]) + wide(branch_parts[1]) + wide(branch_parts[2])
    grad_up, grad_down = up(hat[:cut]), down(hat[cut:])
    for step in range(far - 1, 0, -1):
        a, sums_a = grads(step, hat)
        hat, sums_b = grads(rows - step, a)
        b = hat
        chunk_sums += [sums_a, sums_b]
        if step == far - 1:
            a = jnp.concatenate([wide(a[:cut]) + wide(grad_up), wide(a[cut:])], axis=0)
            b = jnp.concatenate([wide(b[:cut]), wide(b[cut:]) + wide(grad_down)], axis=0)
        else:
            a, b = wide(a) + wide(grad_up), wide(b) + wide(grad_down)
        grad_up, grad_down = up(a.astype(BF)), down(b.astype(BF))
    hat, sums = grads(0, hat)
    chunk_sums.append(sums)
    norm_sums = jnp.stack([sum(parts) for parts in zip(*chunk_sums)])
    merged_b = jnp.sum(grad_merged.astype(F32), axis=0)
    shift_b = jnp.sum(cotangent.astype(F32), axis=(0, 1))
    sums = jnp.concatenate(
        [
            norm_sums.reshape(4, cols, width).transpose(1, 0, 2).reshape(cols, 4 * width),
            jnp.broadcast_to(merged_b, (cols, merged_cols)),
            jnp.broadcast_to(expand_b, (cols, expand_b.shape[0])),
        ],
        axis=1,
    ).reshape(cols, -1, 128)
    branch = col_swap(branch.astype(BF).reshape(block_rows, cols, width).transpose(1, 0, 2))
    spread_sums = lax.all_to_all(
        after(sums, branch), "col", split_axis=0, concat_axis=0, tiled=True
    )
    mix = lax.optimization_barrier((mix, hat))[0]
    output_sent, output_taken = give(cot_other, mix)
    output_dot = keep(cot_own, mix, output_taken)
    output_grad = scatter_weight(after(output_dot, merged_grad)).T
    grad_hat = wide(hat) + wide(grad_up) + wide(grad_down)
    sums = jnp.sum(spread_sums.reshape(cols, -1), axis=0)
    merged_b = sums[4 * width : 4 * width + merged_cols]
    expand_b = sums[4 * width + merged_cols :]
    tail, far_tail = add_up(
        jnp.concatenate([sums[: 4 * width], shift_b]).reshape(-1, 128), "row", rows
    )
    tail = tail.reshape(5, width)
    branch = from_rows(branch)
    result = inputs.astype(F32) + branch.astype(F32) + output_bias + reduce_bias
    result = result.astype(BF)

    part_normed, part_inverse = norm(x_part)
    norm_part = part_inverse * (
        grad_hat
        - jnp.mean(grad_hat, axis=-1, keepdims=True)
        - part_normed * jnp.mean(grad_hat * part_normed, axis=-1, keepdims=True)
    )

    norm_part = after(norm_part.astype(BF), merged_grad, spread_sums)
    norm_part = col_swap(norm_part.reshape(block_rows, cols, width).transpose(1, 0, 2))
    norm_part = from_rows(norm_part, result, far_tail, output_grad)
    input_grad = cotangent.astype(F32) + norm_part.astype(F32)
    norm_sums, shift_b = tail[:4], tail[4]
    return (
        result,
        input_grad,
        norm_sums[0],
        norm_sums[1],
        norm_sums[2],
        norm_sums[3],
        merged_grad,
        merged_b,
        output_grad,
        shift_b,
        expand_grad,
        expand_b,
        reduce_grad,
        shift_b,
    )


def solution(mesh):
    in_specs = (
        P(None, "row", "col"),
        P(None, "col", None),
        P("col"),
        P("col"),
        P("col"),
        P("col"),
        P("col", "row"),
        P("row"),
        P("row", "col"),
        P("col"),
        P("col", "row"),
        P("row"),
        P("row", "col"),
        P("col"),
        P(None, "row", "col"),
    )
    out_specs = (
        P(None, "row", "col"),
        P(None, "row", "col"),
        P("col"),
        P("col"),
        P("col"),
        P("col"),
        P("col", "row"),
        P("row"),
        P("row", "col"),
        P("col"),
        P("col", "row"),
        P("row"),
        P("row", "col"),
        P("col"),
    )
    return jax.shard_map(body, mesh=mesh, in_specs=in_specs, out_specs=out_specs, check_vma=False)
```

```python
import functools

import jax
import jax.numpy as jnp
from jax import lax
from jax.experimental import pallas as pl
from jax.experimental.pallas import tpu as pltpu
from jax.sharding import PartitionSpec as P

D = 2048
HEAD = 256
ROT = 64
L = 1024
PIECE = 256
SPAN = 512

norm_eps = 1e-05
theta_base = 10000.0
BF = jnp.bfloat16
F32 = jnp.float32


def mm(left, right):
    return jnp.dot(left, right, preferred_element_type=F32)


def contract_last(left, right):
    return lax.dot_general(left, right, (((1,), (1,)), ((), ())), preferred_element_type=F32)


def contract_first(left, right):
    return lax.dot_general(left, right, (((0,), (0,)), ((), ())), preferred_element_type=F32)


def rotary_tables():
    half = ROT // 2
    freq_steps = jnp.arange(half, dtype=F32)
    inverse = jnp.power(theta_base, -(2.0 * freq_steps) / ROT)
    angles = jnp.arange(L, dtype=jnp.int32).astype(F32)[:, None] * inverse[None, :]
    cosine = jnp.cos(angles)
    sine = jnp.sin(angles)
    rest = 128 - ROT
    cos_table = jnp.concatenate([cosine, cosine, jnp.ones((L, rest), F32)], axis=1)
    sin_table = jnp.concatenate([-sine, sine, jnp.zeros((L, rest), F32)], axis=1)
    return cos_table, sin_table


def turn(block, cos, sin):
    half = ROT // 2
    head = block[:, :128]
    lane = lax.broadcasted_iota(jnp.int32, head.shape, 1)
    partner = jnp.where(lane < half, pltpu.roll(head, 128 - half, 1), pltpu.roll(head, half, 1))
    return jnp.concatenate([head * cos + partner * sin, block[:, 128:]], axis=1)


def attention_kernel(
    slot_ref, starts_ref, pre_ref, gm_ref, cos_ref, sin_ref,
    mix_ref, grad_ref, q_s, k_s, v_s, g_s, gk_s, gv_s, *, parts, part,
):
    m = pl.program_id(1)
    scale = HEAD ** (-0.5)
    for a in range(parts):
        rows = slice(a * part, (a + 1) * part)
        j = slot_ref[a]
        block = pre_ref[j, 0]
        cos, sin = cos_ref[rows], sin_ref[rows]
        q_s[rows] = turn(block[:, :HEAD], cos, sin).astype(BF)
        k_s[rows] = turn(block[:, HEAD : 2 * HEAD], cos, sin).astype(BF)
        v_s[rows] = block[:, 2 * HEAD :].astype(BF)
        g_s[rows] = gm_ref[j, 0]
    for first in range(0, L, SPAN):
        last = first + SPAN
        q, g = q_s[first:last], g_s[first:last]
        k, v = k_s[:last], v_s[:last]
        row = lax.broadcasted_iota(jnp.int32, (SPAN, 1), 0) + first
        limit = row
        for piece in range(2):
            low = starts_ref[2 * m + piece]
            limit = jnp.where((row >= low) & (row < low + PIECE), low + PIECE - 1, limit)
        column = lax.broadcasted_iota(jnp.int32, (SPAN, last), 1)
        scores = jnp.where(column <= limit, contract_last(q, k) * scale, -jnp.inf)
        top = jnp.max(scores, axis=1, keepdims=True)
        powers = jnp.exp(scores - top)
        probs = powers * (1.0 / jnp.sum(powers, axis=1, keepdims=True))
        pb = probs.astype(BF)
        mix = mm(pb, v).astype(BF)
        gp = contract_last(g, v)
        delta = jnp.sum(gp * probs, axis=1, keepdims=True)
        gs = (probs * (gp - delta)).astype(BF)
        gq = mm(gs, k) * scale
        gk = contract_first(gs, q)
        gv = contract_first(pb, g)
        if first == 0:
            gk_s[:last] = gk
            gv_s[:last] = gv
            gk_s[last:] = jnp.zeros((L - last, HEAD), F32)
            gv_s[last:] = jnp.zeros((L - last, HEAD), F32)
        else:
            gk_s[:last] += gk
            gv_s[:last] += gv
        for a in range(first // part, last // part):
            rows = slice(a * part - first, (a + 1) * part - first)
            table = slice(a * part, (a + 1) * part)
            j = slot_ref[a]
            mix_ref[j, 0] = mix[rows]
            grad_ref[j, 0, :, :HEAD] = turn(gq[rows], cos_ref[table], -sin_ref[table]).astype(BF)
    for a in range(parts):
        rows = slice(a * part, (a + 1) * part)
        j = slot_ref[a]
        gk = gk_s[rows] * scale
        grad_ref[j, 0, :, HEAD : 2 * HEAD] = turn(gk, cos_ref[rows], -sin_ref[rows]).astype(BF)
        grad_ref[j, 0, :, 2 * HEAD :] = gv_s[rows].astype(BF)


def attention(slots, starts, merged_pre, grad_mix, tables, micro, parts):
    part = L // parts
    heads = merged_pre.shape[1] // (3 * HEAD)
    cos, sin = tables
    pre = merged_pre.reshape(parts, micro, part, heads * 3 * HEAD)
    gm = grad_mix.reshape(parts, micro, part, heads * HEAD)
    spec = lambda w: pl.BlockSpec((parts, 1, part, w), lambda h, m, *_: (0, m, 0, h))
    table = pl.BlockSpec((L, 128), lambda h, m, *_: (0, 0))
    flops = heads * micro * 2 * 5 * L * L * HEAD * 3 // 4
    mix, grads = pl.pallas_call(
        functools.partial(attention_kernel, parts=parts, part=part),
        out_shape=(
            jax.ShapeDtypeStruct(gm.shape, BF),
            jax.ShapeDtypeStruct(pre.shape, BF),
        ),
        grid_spec=pltpu.PrefetchScalarGridSpec(
            num_scalar_prefetch=2,
            grid=(heads, micro),
            in_specs=[spec(3 * HEAD), spec(HEAD), table, table],
            out_specs=[spec(HEAD), spec(3 * HEAD)],
            scratch_shapes=[pltpu.VMEM((L, HEAD), BF)] * 4 + [pltpu.VMEM((L, HEAD), F32)] * 2,
        ),
        compiler_params=pltpu.CompilerParams(
            dimension_semantics=("arbitrary", "arbitrary"), vmem_limit_bytes=60 << 20
        ),
        cost_estimate=pl.CostEstimate(
            flops=2 * flops, bytes_accessed=pre.size * 6 + gm.size * 4, transcendentals=heads * micro * L * L
        ),
        name="attention",
    )(slots, starts, pre, gm, cos, sin)
    return mix.reshape(-1, heads * HEAD), grads.reshape(-1, heads * 3 * HEAD)


def after(value, *earlier):
    return lax.optimization_barrier((value,) + earlier)[0]


def ring_order(rows):
    if rows < 4:
        return list(range(rows))
    half = rows // 2
    return list(range(half)) + list(range(rows - 1, half - 1, -1))


def body(
    inputs,
    piece_starts,
    first_gain,
    first_shift,
    second_gain,
    second_shift,
    merged_weight,
    merged_bias,
    output_weight,
    output_bias,
    expand_weight,
    expand_bias,
    reduce_weight,
    reduce_bias,
    cotangent,
):
    rows = lax.axis_size("row")
    cols = lax.axis_size("col")
    micro, own_tokens, width = inputs.shape
    per_row = own_tokens // L
    part = L // rows
    block_rows = micro * part
    order = ring_order(rows)
    spot = [order.index(r) for r in range(rows)]
    ahead = [(order[i], order[(i + 1) % rows]) for i in range(rows)]
    behind = [(b, a) for a, b in ahead]
    me = lax.axis_index("row")
    my_spot = jnp.asarray(spot, jnp.int32)[me]
    slots = (jnp.asarray(spot, jnp.int32) - my_spot) % rows
    up = lambda v: lax.ppermute(v, "row", ahead)
    down = lambda v: lax.ppermute(v, "row", behind)

    def row_swap(own):
        b = own.reshape(micro, per_row, rows, part, width).transpose(2, 1, 0, 3, 4)
        b = lax.all_to_all(b, "row", split_axis=0, concat_axis=0, tiled=True)
        return b.reshape(rows * per_row, block_rows, width)

    def col_swap(b):
        return lax.all_to_all(b, "col", split_axis=0, concat_axis=0, tiled=True)

    def side_by_side(b):
        return b.transpose(1, 0, 2).reshape(block_rows, cols * width)

    def from_rows(block, *earlier):
        b = block.reshape(rows, per_row, micro, part, width)
        if earlier:
            b = lax.all_to_all(after(b, *earlier), "row", split_axis=0, concat_axis=0, tiled=True)
            return b.transpose(2, 1, 0, 3, 4).reshape(micro, own_tokens, width)
        b = b.transpose(0, 2, 1, 3, 4)
        whole = jnp.zeros((micro, per_row, rows, part, width), BF)
        for step in range(rows):
            other = partner(me, step)
            source = me ^ step if rows & (rows - 1) == 0 else (me - step) % rows
            piece = lax.dynamic_index_in_dim(b, other, 0, keepdims=False)
            if step:
                piece = lax.ppermute(piece, "row", [(r, partner(r, step)) for r in range(rows)])
            whole = lax.dynamic_update_slice_in_dim(whole, piece[:, :, None], source, 2)
        return whole.reshape(micro, own_tokens, width)

    def partner(r, step):
        return r ^ step if rows & (rows - 1) == 0 else (r + step) % rows

    far = rows // 2
    cut = block_rows // 2

    def ring_gather(own, *earlier):
        pieces = [None] * rows
        pieces[0] = own
        fore, back = own, own
        for step in range(1, far):
            fore, back = up(fore), down(back)
            pieces[rows - step], pieces[step] = fore, back
        if earlier:
            fore, back = lax.optimization_barrier((fore, back) + earlier)[:2]
        pieces[far] = jnp.concatenate([up(fore[:cut]), down(back[cut:])], axis=0)
        return jnp.concatenate(pieces, axis=0)

    def chunk(total, j):
        return total[j * block_rows : (j + 1) * block_rows]

    def ring_open(total):
        last = chunk(total, far)
        return up(last[:cut]), down(last[cut:])

    def ring_close(total, halves):
        half_up, half_down = halves
        fore = back = None
        for step in range(far - 1, 0, -1):
            a, b = chunk(total, step).astype(F32), chunk(total, rows - step).astype(F32)
            if fore is None:
                a = jnp.concatenate([a[:cut] + half_up.astype(F32), a[cut:]], axis=0)
                b = jnp.concatenate([b[:cut], b[cut:] + half_down.astype(F32)], axis=0)
            else:
                a, b = a + fore.astype(F32), b + back.astype(F32)
            fore, back = up(a.astype(BF)), down(b.astype(BF))
        return chunk(total, 0).astype(F32) + fore.astype(F32) + back.astype(F32)

    def norm(block):
        block = block.astype(F32)
        center = jnp.mean(block, axis=-1, keepdims=True)
        spread = jnp.mean((block - center) ** 2, axis=-1, keepdims=True)
        inverse_std = lax.rsqrt(spread + norm_eps)
        return (block - center) * inverse_std, inverse_std

    def broadcast(value, axis, size):
        return lax.all_to_all(
            jnp.broadcast_to(value, (size,) + value.shape), axis, split_axis=0, concat_axis=0, tiled=True
        )

    gains = jnp.stack([first_gain, first_shift, second_gain, second_shift])
    spread_gains = broadcast(gains, "col", cols)
    gains = spread_gains.transpose(1, 0, 2).reshape(4, cols * width)
    expand_w = lax.all_gather(expand_weight, "col", axis=0, tiled=True)
    x_half = row_swap(after(inputs, spread_gains))
    cot_half = row_swap(after(cotangent, x_half))
    x_part = col_swap(after(x_half, cot_half))
    reduce_w = lax.all_gather(after(reduce_weight, x_part), "col", axis=1, tiled=True)
    mixed_weight = jnp.concatenate([merged_weight, output_weight.T], axis=1)
    cot_part = col_swap(after(cot_half, x_part))
    merged_cols = merged_weight.shape[1]
    x_part = side_by_side(x_part)
    x_seq = ring_gather(x_part)

    normed, _ = norm(x_seq)
    attend_in = (normed * gains[0] + gains[1]).astype(BF)
    expand_in = (normed * gains[2] + gains[3]).astype(BF)

    expand_pre = lax.optimization_barrier(mm(expand_in, expand_w) + expand_bias)
    cot_part = side_by_side(after(cot_part, expand_pre[:8, :128]))
    mixed_w = lax.all_gather(after(mixed_weight, cot_part), "col", axis=0, tiled=True)
    merged_w, output_wt = mixed_w[:, :merged_cols], mixed_w[:, merged_cols:]
    phi_sum = 0.5 * (1.0 + lax.erf(expand_pre * (0.5 ** 0.5)))
    density = jnp.exp(-0.5 * expand_pre * expand_pre) * 0.3989422804014327
    activated = (expand_pre * phi_sum).astype(BF)
    slope = (phi_sum + expand_pre * density).astype(BF)
    activated, slope = lax.optimization_barrier((activated, slope))
    cot_seq = ring_gather(cot_part, activated)

    def scatter_weight(grad):
        return lax.psum_scatter(grad, "col", scatter_dimension=0, tiled=True).astype(F32)

    cot_seq, attend_in, *tables = lax.optimization_barrier(
        (cot_seq, attend_in) + rotary_tables()
    )
    reduce_dot = contract_first(cot_seq, activated).astype(BF)
    reduce_grad = scatter_weight(reduce_dot).T
    grad_act = contract_last(after(cot_seq, reduce_dot), reduce_w)
    grad_pre = (grad_act * slope.astype(F32)).astype(BF)
    expand_b = jnp.sum(grad_pre.astype(F32), axis=0)
    expand_dot = contract_first(expand_in, grad_pre).astype(BF)
    expand_grad = scatter_weight(expand_dot)

    branch_ff = mm(after(activated, expand_dot), reduce_w).astype(BF)
    merged_pre = mm(after(attend_in, expand_dot), merged_w) + merged_bias
    grad_mix = mm(after(cot_seq, expand_dot), output_wt).astype(BF)
    mix, grad_merged = attention(
        slots, piece_starts.reshape(-1), merged_pre, grad_mix, tables, micro, rows
    )
    branch = (contract_last(mix, output_wt) + branch_ff).astype(BF)
    halves = ring_open(branch)
    grad_merged, attend_late = lax.optimization_barrier(
        (grad_merged, attend_in, branch, reduce_grad)
    )[:2]
    merged_dot = contract_first(attend_late, grad_merged).astype(BF)
    merged_grad = scatter_weight(merged_dot)
    grad_merged, grad_pre, half_up, half_down = lax.optimization_barrier(
        (grad_merged, grad_pre) + halves + (merged_dot,)
    )[:4]
    branch = ring_close(branch, (half_up, half_down))
    grad_first = contract_last(grad_merged, merged_w)
    grad_second = contract_last(grad_pre, expand_w)
    norm_sums = jnp.stack(
        [
            jnp.sum(grad_first * normed, axis=0),
            jnp.sum(grad_first, axis=0),
            jnp.sum(grad_second * normed, axis=0),
            jnp.sum(grad_second, axis=0),
        ]
    )
    grad_hat = (grad_first * gains[0] + grad_second * gains[2]).astype(BF)
    grad_hat = after(grad_hat, expand_grad)
    halves = ring_open(grad_hat)
    merged_b = jnp.sum(grad_merged.astype(F32), axis=0)
    shift_b = jnp.sum(cotangent.astype(F32), axis=(0, 1))
    sums = jnp.concatenate(
        [
            norm_sums.reshape(4, cols, width).transpose(1, 0, 2).reshape(cols, 4 * width),
            jnp.broadcast_to(merged_b, (cols, merged_cols)),
            jnp.broadcast_to(expand_b, (cols, expand_b.shape[0])),
        ],
        axis=1,
    ).reshape(cols, -1, 128)
    branch = col_swap(branch.astype(BF).reshape(block_rows, cols, width).transpose(1, 0, 2))
    spread_sums = lax.all_to_all(
        after(sums, branch), "col", split_axis=0, concat_axis=0, tiled=True
    )
    grad_hat = ring_close(grad_hat, halves)
    sums = jnp.sum(spread_sums.reshape(cols, -1), axis=0)
    merged_b = sums[4 * width : 4 * width + merged_cols]
    expand_b = sums[4 * width + merged_cols :]
    tail = jnp.concatenate([sums[: 4 * width], shift_b]).reshape(-1, 128)
    if rows & (rows - 1) == 0:
        step = 1
        while step < rows:
            far_tail = lax.ppermute(tail, "row", [(r, r ^ step) for r in range(rows)])
            tail = tail + far_tail
            step *= 2
    else:
        far_tail = broadcast(tail, "row", rows)
        tail = jnp.sum(far_tail, axis=0)
    tail = tail.reshape(5, width)
    branch = from_rows(branch)
    result = inputs.astype(F32) + branch.astype(F32) + output_bias + reduce_bias
    result = result.astype(BF)

    part_normed, part_inverse = norm(x_part)
    norm_part = part_inverse * (
        grad_hat
        - jnp.mean(grad_hat, axis=-1, keepdims=True)
        - part_normed * jnp.mean(grad_hat * part_normed, axis=-1, keepdims=True)
    )

    norm_part = after(norm_part.astype(BF), merged_grad, spread_sums)
    norm_part = col_swap(norm_part.reshape(block_rows, cols, width).transpose(1, 0, 2))
    mix_late, cot_late = lax.optimization_barrier((mix, cot_seq, grad_hat, far_tail))[:2]
    output_dot = contract_first(cot_late, mix_late).astype(BF)
    output_grad = scatter_weight(after(output_dot, norm_part)).T
    input_grad = cotangent.astype(F32) + from_rows(norm_part, result, output_dot).astype(F32)
    norm_sums, shift_b = tail[:4], tail[4]
    return (
        result,
        input_grad,
        norm_sums[0],
        norm_sums[1],
        norm_sums[2],
        norm_sums[3],
        merged_grad,
        merged_b,
        output_grad,
        shift_b,
        expand_grad,
        expand_b,
        reduce_grad,
        shift_b,
    )


def solution(mesh):
    in_specs = (
        P(None, "row", "col"),
        P(None, "col", None),
        P("col"),
        P("col"),
        P("col"),
        P("col"),
        P("col", "row"),
        P("row"),
        P("row", "col"),
        P("col"),
        P("col", "row"),
        P("row"),
        P("row", "col"),
        P("col"),
        P(None, "row", "col"),
    )
    out_specs = (
        P(None, "row", "col"),
        P(None, "row", "col"),
        P("col"),
        P("col"),
        P("col"),
        P("col"),
        P("col", "row"),
        P("row"),
        P("row", "col"),
        P("col"),
        P("col", "row"),
        P("row"),
        P("row", "col"),
        P("col"),
    )
    return jax.shard_map(body, mesh=mesh, in_specs=in_specs, out_specs=out_specs, check_vma=False)
```

```python
import functools

import jax
import jax.numpy as jnp
from jax import lax
from jax.experimental import pallas as pl
from jax.experimental.pallas import tpu as pltpu
from jax.sharding import PartitionSpec as P

D = 2048
HEAD = 256
ROT = 64
L = 1024
PIECE = 256
SPAN = 512

norm_eps = 1e-05
theta_base = 10000.0
BF = jnp.bfloat16
F32 = jnp.float32


def mm(left, right):
    return jnp.dot(left, right, preferred_element_type=F32)


def contract_last(left, right):
    return lax.dot_general(left, right, (((1,), (1,)), ((), ())), preferred_element_type=F32)


def contract_first(left, right):
    return lax.dot_general(left, right, (((0,), (0,)), ((), ())), preferred_element_type=F32)


def rotary_tables():
    half = ROT // 2
    freq_steps = jnp.arange(half, dtype=F32)
    inverse = jnp.power(theta_base, -(2.0 * freq_steps) / ROT)
    angles = jnp.arange(L, dtype=jnp.int32).astype(F32)[:, None] * inverse[None, :]
    cosine = jnp.cos(angles)
    sine = jnp.sin(angles)
    rest = 128 - ROT
    cos_table = jnp.concatenate([cosine, cosine, jnp.ones((L, rest), F32)], axis=1)
    sin_table = jnp.concatenate([-sine, sine, jnp.zeros((L, rest), F32)], axis=1)
    return cos_table, sin_table


def turn(block, cos, sin):
    half = ROT // 2
    head = block[:, :128]
    lane = lax.broadcasted_iota(jnp.int32, head.shape, 1)
    partner = jnp.where(lane < half, pltpu.roll(head, 128 - half, 1), pltpu.roll(head, half, 1))
    return jnp.concatenate([head * cos + partner * sin, block[:, 128:]], axis=1)


def attention_kernel(
    slot_ref, starts_ref, pre_ref, gm_ref, cos_ref, sin_ref,
    mix_ref, grad_ref, q_s, k_s, v_s, g_s, gk_s, gv_s, *, parts, part,
):
    m = pl.program_id(1)
    scale = HEAD ** (-0.5)
    for a in range(parts):
        rows = slice(a * part, (a + 1) * part)
        j = slot_ref[a]
        block = pre_ref[j, 0]
        cos, sin = cos_ref[rows], sin_ref[rows]
        q_s[rows] = turn(block[:, :HEAD], cos, sin).astype(BF)
        k_s[rows] = turn(block[:, HEAD : 2 * HEAD], cos, sin).astype(BF)
        v_s[rows] = block[:, 2 * HEAD :].astype(BF)
        g_s[rows] = gm_ref[j, 0]
    for first in range(0, L, SPAN):
        last = first + SPAN
        q, g = q_s[first:last], g_s[first:last]
        k, v = k_s[:last], v_s[:last]
        row = lax.broadcasted_iota(jnp.int32, (SPAN, 1), 0) + first
        limit = row
        for piece in range(2):
            low = starts_ref[2 * m + piece]
            limit = jnp.where((row >= low) & (row < low + PIECE), low + PIECE - 1, limit)
        column = lax.broadcasted_iota(jnp.int32, (SPAN, last), 1)
        scores = jnp.where(column <= limit, contract_last(q, k) * scale, -jnp.inf)
        top = jnp.max(scores, axis=1, keepdims=True)
        powers = jnp.exp(scores - top)
        probs = powers * (1.0 / jnp.sum(powers, axis=1, keepdims=True))
        pb = probs.astype(BF)
        mix = mm(pb, v).astype(BF)
        gp = contract_last(g, v)
        delta = jnp.sum(gp * probs, axis=1, keepdims=True)
        gs = (probs * (gp - delta)).astype(BF)
        gq = mm(gs, k) * scale
        gk = contract_first(gs, q)
        gv = contract_first(pb, g)
        if first == 0:
            gk_s[:last] = gk
            gv_s[:last] = gv
            gk_s[last:] = jnp.zeros((L - last, HEAD), F32)
            gv_s[last:] = jnp.zeros((L - last, HEAD), F32)
        else:
            gk_s[:last] += gk
            gv_s[:last] += gv
        for a in range(first // part, last // part):
            rows = slice(a * part - first, (a + 1) * part - first)
            table = slice(a * part, (a + 1) * part)
            j = slot_ref[a]
            mix_ref[j, 0] = mix[rows]
            grad_ref[j, 0, :, :HEAD] = turn(gq[rows], cos_ref[table], -sin_ref[table]).astype(BF)
    for a in range(parts):
        rows = slice(a * part, (a + 1) * part)
        j = slot_ref[a]
        gk = gk_s[rows] * scale
        grad_ref[j, 0, :, HEAD : 2 * HEAD] = turn(gk, cos_ref[rows], -sin_ref[rows]).astype(BF)
        grad_ref[j, 0, :, 2 * HEAD :] = gv_s[rows].astype(BF)


def attention(slots, starts, merged_pre, grad_mix, tables, micro, parts):
    part = L // parts
    heads = merged_pre.shape[1] // (3 * HEAD)
    cos, sin = tables
    pre = merged_pre.reshape(parts, micro, part, heads * 3 * HEAD)
    gm = grad_mix.reshape(parts, micro, part, heads * HEAD)
    spec = lambda w: pl.BlockSpec((parts, 1, part, w), lambda h, m, *_: (0, m, 0, h))
    table = pl.BlockSpec((L, 128), lambda h, m, *_: (0, 0))
    flops = heads * micro * 2 * 5 * L * L * HEAD * 3 // 4
    mix, grads = pl.pallas_call(
        functools.partial(attention_kernel, parts=parts, part=part),
        out_shape=(
            jax.ShapeDtypeStruct(gm.shape, BF),
            jax.ShapeDtypeStruct(pre.shape, BF),
        ),
        grid_spec=pltpu.PrefetchScalarGridSpec(
            num_scalar_prefetch=2,
            grid=(heads, micro),
            in_specs=[spec(3 * HEAD), spec(HEAD), table, table],
            out_specs=[spec(HEAD), spec(3 * HEAD)],
            scratch_shapes=[pltpu.VMEM((L, HEAD), BF)] * 4 + [pltpu.VMEM((L, HEAD), F32)] * 2,
        ),
        compiler_params=pltpu.CompilerParams(
            dimension_semantics=("arbitrary", "arbitrary"), vmem_limit_bytes=60 << 20
        ),
        cost_estimate=pl.CostEstimate(
            flops=2 * flops, bytes_accessed=pre.size * 6 + gm.size * 4, transcendentals=heads * micro * L * L
        ),
        name="attention",
    )(slots, starts, pre, gm, cos, sin)
    return mix.reshape(-1, heads * HEAD), grads.reshape(-1, heads * 3 * HEAD)


def after(value, *earlier):
    return lax.optimization_barrier((value,) + earlier)[0]


def ring_order(rows):
    if rows < 4:
        return list(range(rows))
    half = rows // 2
    return list(range(half)) + list(range(rows - 1, half - 1, -1))


def body(
    inputs,
    piece_starts,
    first_gain,
    first_shift,
    second_gain,
    second_shift,
    merged_weight,
    merged_bias,
    output_weight,
    output_bias,
    expand_weight,
    expand_bias,
    reduce_weight,
    reduce_bias,
    cotangent,
):
    rows = lax.axis_size("row")
    cols = lax.axis_size("col")
    micro, own_tokens, width = inputs.shape
    per_row = own_tokens // L
    part = L // rows
    block_rows = micro * part
    order = ring_order(rows)
    spot = [order.index(r) for r in range(rows)]
    ahead = [(order[i], order[(i + 1) % rows]) for i in range(rows)]
    behind = [(b, a) for a, b in ahead]
    me = lax.axis_index("row")
    my_spot = jnp.asarray(spot, jnp.int32)[me]
    slots = (jnp.asarray(spot, jnp.int32) - my_spot) % rows
    up = lambda v: lax.ppermute(v, "row", ahead)
    down = lambda v: lax.ppermute(v, "row", behind)

    def row_swap(own):
        b = own.reshape(micro, per_row, rows, part, width).transpose(2, 1, 0, 3, 4)
        b = lax.all_to_all(b, "row", split_axis=0, concat_axis=0, tiled=True)
        return b.reshape(rows * per_row, block_rows, width)

    def col_swap(b):
        return lax.all_to_all(b, "col", split_axis=0, concat_axis=0, tiled=True)

    def side_by_side(b):
        return b.transpose(1, 0, 2).reshape(block_rows, cols * width)

    def from_rows(block, *earlier):
        b = block.reshape(rows, per_row, micro, part, width)
        if earlier:
            b = lax.all_to_all(after(b, *earlier), "row", split_axis=0, concat_axis=0, tiled=True)
            return b.transpose(2, 1, 0, 3, 4).reshape(micro, own_tokens, width)
        b = b.transpose(0, 2, 1, 3, 4)
        whole = jnp.zeros((micro, per_row, rows, part, width), BF)
        for step in range(rows):
            other = partner(me, step)
            source = me ^ step if rows & (rows - 1) == 0 else (me - step) % rows
            piece = lax.dynamic_index_in_dim(b, other, 0, keepdims=False)
            if step:
                piece = lax.ppermute(piece, "row", [(r, partner(r, step)) for r in range(rows)])
            whole = lax.dynamic_update_slice_in_dim(whole, piece[:, :, None], source, 2)
        return whole.reshape(micro, own_tokens, width)

    def partner(r, step):
        return r ^ step if rows & (rows - 1) == 0 else (r + step) % rows

    far = rows // 2
    cut = block_rows // 2

    def ring_gather(own, *earlier):
        pieces = [None] * rows
        pieces[0] = own
        fore, back = own, own
        for step in range(1, far):
            fore, back = up(fore), down(back)
            pieces[rows - step], pieces[step] = fore, back
        if earlier:
            fore, back = lax.optimization_barrier((fore, back) + earlier)[:2]
        pieces[far] = jnp.concatenate([up(fore[:cut]), down(back[cut:])], axis=0)
        return jnp.concatenate(pieces, axis=0)

    def chunk(total, j):
        return total[j * block_rows : (j + 1) * block_rows]

    def ring_open(total):
        last = chunk(total, far)
        return up(last[:cut]), down(last[cut:])

    def ring_close(total, halves):
        half_up, half_down = halves
        fore = back = None
        for step in range(far - 1, 0, -1):
            a, b = chunk(total, step).astype(F32), chunk(total, rows - step).astype(F32)
            if fore is None:
                a = jnp.concatenate([a[:cut] + half_up.astype(F32), a[cut:]], axis=0)
                b = jnp.concatenate([b[:cut], b[cut:] + half_down.astype(F32)], axis=0)
            else:
                a, b = a + fore.astype(F32), b + back.astype(F32)
            fore, back = up(a.astype(BF)), down(b.astype(BF))
        return chunk(total, 0).astype(F32) + fore.astype(F32) + back.astype(F32)

    def norm(block):
        block = block.astype(F32)
        center = jnp.mean(block, axis=-1, keepdims=True)
        spread = jnp.mean((block - center) ** 2, axis=-1, keepdims=True)
        inverse_std = lax.rsqrt(spread + norm_eps)
        return (block - center) * inverse_std, inverse_std

    def broadcast(value, axis, size):
        return lax.all_to_all(
            jnp.broadcast_to(value, (size,) + value.shape), axis, split_axis=0, concat_axis=0, tiled=True
        )

    gains = jnp.stack([first_gain, first_shift, second_gain, second_shift])
    spread_gains = broadcast(gains, "col", cols)
    gains = spread_gains.transpose(1, 0, 2).reshape(4, cols * width)
    expand_w = lax.all_gather(expand_weight, "col", axis=0, tiled=True)
    x_half = row_swap(after(inputs, spread_gains))
    cot_half = row_swap(after(cotangent, x_half))
    x_part = col_swap(after(x_half, cot_half))
    reduce_w = lax.all_gather(after(reduce_weight, x_part), "col", axis=1, tiled=True)
    mixed_weight = jnp.concatenate([merged_weight, output_weight.T], axis=1)
    cot_part = col_swap(after(cot_half, x_part))
    merged_cols = merged_weight.shape[1]
    x_part = side_by_side(x_part)
    x_seq = ring_gather(x_part)

    normed, _ = norm(x_seq)
    attend_in = (normed * gains[0] + gains[1]).astype(BF)
    expand_in = (normed * gains[2] + gains[3]).astype(BF)

    expand_pre = lax.optimization_barrier(mm(expand_in, expand_w) + expand_bias)
    cot_part = side_by_side(after(cot_part, expand_pre[:8, :128]))
    mixed_w = lax.all_gather(after(mixed_weight, cot_part), "col", axis=0, tiled=True)
    merged_w, output_wt = mixed_w[:, :merged_cols], mixed_w[:, merged_cols:]
    phi_sum = 0.5 * (1.0 + lax.erf(expand_pre * (0.5 ** 0.5)))
    density = jnp.exp(-0.5 * expand_pre * expand_pre) * 0.3989422804014327
    activated = (expand_pre * phi_sum).astype(BF)
    slope = (phi_sum + expand_pre * density).astype(BF)
    activated, slope = lax.optimization_barrier((activated, slope))
    branch_ff = mm(activated, reduce_w).astype(BF)
    cot_seq = ring_gather(cot_part, branch_ff)

    def scatter_weight(grad):
        return lax.psum_scatter(grad, "col", scatter_dimension=0, tiled=True).astype(F32)

    cot_seq, branch_ff, attend_in, *tables = lax.optimization_barrier(
        (cot_seq, branch_ff, attend_in) + rotary_tables()
    )
    reduce_dot = contract_first(cot_seq, activated).astype(BF)
    reduce_grad = scatter_weight(reduce_dot).T
    grad_act = contract_last(after(cot_seq, reduce_dot), reduce_w)
    grad_pre = (grad_act * slope.astype(F32)).astype(BF)
    expand_b = jnp.sum(grad_pre.astype(F32), axis=0)
    expand_dot = contract_first(expand_in, grad_pre).astype(BF)
    expand_grad = scatter_weight(expand_dot)

    merged_pre = mm(after(attend_in, expand_dot), merged_w) + merged_bias
    grad_mix = mm(after(cot_seq, expand_dot), output_wt).astype(BF)
    mix, grad_merged = attention(
        slots, piece_starts.reshape(-1), merged_pre, grad_mix, tables, micro, rows
    )
    branch = (contract_last(mix, output_wt) + branch_ff).astype(BF)
    halves = ring_open(branch)
    grad_merged, attend_late = lax.optimization_barrier(
        (grad_merged, attend_in, branch, reduce_grad)
    )[:2]
    merged_dot = contract_first(attend_late, grad_merged).astype(BF)
    merged_grad = scatter_weight(merged_dot)
    grad_merged, grad_pre, half_up, half_down = lax.optimization_barrier(
        (grad_merged, grad_pre) + halves + (merged_dot,)
    )[:4]
    branch = ring_close(branch, (half_up, half_down))
    grad_first = contract_last(grad_merged, merged_w)
    grad_second = contract_last(grad_pre, expand_w)
    norm_sums = jnp.stack(
        [
            jnp.sum(grad_first * normed, axis=0),
            jnp.sum(grad_first, axis=0),
            jnp.sum(grad_second * normed, axis=0),
            jnp.sum(grad_second, axis=0),
        ]
    )
    grad_hat = (grad_first * gains[0] + grad_second * gains[2]).astype(BF)
    halves = ring_open(grad_hat)
    merged_b = jnp.sum(grad_merged.astype(F32), axis=0)
    shift_b = jnp.sum(cotangent.astype(F32), axis=(0, 1))
    sums = jnp.concatenate(
        [
            norm_sums.reshape(4, cols, width).transpose(1, 0, 2).reshape(cols, 4 * width),
            jnp.broadcast_to(merged_b, (cols, merged_cols)),
            jnp.broadcast_to(expand_b, (cols, expand_b.shape[0])),
        ],
        axis=1,
    ).reshape(cols, -1, 128)
    branch = col_swap(branch.astype(BF).reshape(block_rows, cols, width).transpose(1, 0, 2))
    spread_sums = lax.all_to_all(
        after(sums, branch), "col", split_axis=0, concat_axis=0, tiled=True
    )
    halves = lax.optimization_barrier(halves + (expand_grad,))[:2]
    grad_hat = ring_close(grad_hat, halves)
    sums = jnp.sum(spread_sums.reshape(cols, -1), axis=0)
    merged_b = sums[4 * width : 4 * width + merged_cols]
    expand_b = sums[4 * width + merged_cols :]
    tail = jnp.concatenate([sums[: 4 * width], shift_b]).reshape(-1, 128)
    if rows & (rows - 1) == 0:
        step = 1
        while step < rows:
            far_tail = lax.ppermute(tail, "row", [(r, r ^ step) for r in range(rows)])
            tail = tail + far_tail
            step *= 2
    else:
        far_tail = broadcast(tail, "row", rows)
        tail = jnp.sum(far_tail, axis=0)
    tail = tail.reshape(5, width)
    branch = from_rows(branch)
    result = inputs.astype(F32) + branch.astype(F32) + output_bias + reduce_bias
    result = result.astype(BF)

    part_normed, part_inverse = norm(x_part)
    norm_part = part_inverse * (
        grad_hat
        - jnp.mean(grad_hat, axis=-1, keepdims=True)
        - part_normed * jnp.mean(grad_hat * part_normed, axis=-1, keepdims=True)
    )

    norm_part = after(norm_part.astype(BF), merged_grad, spread_sums)
    norm_part = col_swap(norm_part.reshape(block_rows, cols, width).transpose(1, 0, 2))
    mix_late, cot_late = lax.optimization_barrier((mix, cot_seq, grad_hat, far_tail))[:2]
    output_dot = contract_first(cot_late, mix_late).astype(BF)
    output_grad = scatter_weight(after(output_dot, norm_part)).T
    input_grad = cotangent.astype(F32) + from_rows(norm_part, result, output_dot).astype(F32)
    norm_sums, shift_b = tail[:4], tail[4]
    return (
        result,
        input_grad,
        norm_sums[0],
        norm_sums[1],
        norm_sums[2],
        norm_sums[3],
        merged_grad,
        merged_b,
        output_grad,
        shift_b,
        expand_grad,
        expand_b,
        reduce_grad,
        shift_b,
    )


def solution(mesh):
    in_specs = (
        P(None, "row", "col"),
        P(None, "col", None),
        P("col"),
        P("col"),
        P("col"),
        P("col"),
        P("col", "row"),
        P("row"),
        P("row", "col"),
        P("col"),
        P("col", "row"),
        P("row"),
        P("row", "col"),
        P("col"),
        P(None, "row", "col"),
    )
    out_specs = (
        P(None, "row", "col"),
        P(None, "row", "col"),
        P("col"),
        P("col"),
        P("col"),
        P("col"),
        P("col", "row"),
        P("row"),
        P("row", "col"),
        P("col"),
        P("col", "row"),
        P("row"),
        P("row", "col"),
        P("col"),
    )
    return jax.shard_map(body, mesh=mesh, in_specs=in_specs, out_specs=out_specs, check_vma=False)
```

```python
import functools

import jax
import jax.numpy as jnp
from jax import lax
from jax.experimental import pallas as pl
from jax.experimental.pallas import tpu as pltpu
from jax.sharding import PartitionSpec as P

D = 2048
HEAD = 256
ROT = 64
L = 1024
PIECE = 256
SPAN = 512

norm_eps = 1e-05
theta_base = 10000.0
BF = jnp.bfloat16
F32 = jnp.float32


def mm(left, right):
    return jnp.dot(left, right, preferred_element_type=F32)


def contract_last(left, right):
    return lax.dot_general(left, right, (((1,), (1,)), ((), ())), preferred_element_type=F32)


def contract_first(left, right):
    return lax.dot_general(left, right, (((0,), (0,)), ((), ())), preferred_element_type=F32)


def rotary_tables():
    half = ROT // 2
    freq_steps = jnp.arange(half, dtype=F32)
    inverse = jnp.power(theta_base, -(2.0 * freq_steps) / ROT)
    angles = jnp.arange(L, dtype=jnp.int32).astype(F32)[:, None] * inverse[None, :]
    cosine = jnp.cos(angles)
    sine = jnp.sin(angles)
    rest = 128 - ROT
    cos_table = jnp.concatenate([cosine, cosine, jnp.ones((L, rest), F32)], axis=1)
    sin_table = jnp.concatenate([-sine, sine, jnp.zeros((L, rest), F32)], axis=1)
    return cos_table, sin_table


def turn(block, cos, sin):
    half = ROT // 2
    head = block[:, :128]
    lane = lax.broadcasted_iota(jnp.int32, head.shape, 1)
    partner = jnp.where(lane < half, pltpu.roll(head, 128 - half, 1), pltpu.roll(head, half, 1))
    return jnp.concatenate([head * cos + partner * sin, block[:, 128:]], axis=1)


def attention_kernel(
    slot_ref, starts_ref, pre_ref, gm_ref, cos_ref, sin_ref,
    mix_ref, grad_ref, q_s, k_s, v_s, g_s, gk_s, gv_s, *, parts, part,
):
    m = pl.program_id(1)
    scale = HEAD ** (-0.5)
    for a in range(parts):
        rows = slice(a * part, (a + 1) * part)
        j = slot_ref[a]
        block = pre_ref[j, 0]
        cos, sin = cos_ref[rows], sin_ref[rows]
        q_s[rows] = turn(block[:, :HEAD], cos, sin).astype(BF)
        k_s[rows] = turn(block[:, HEAD : 2 * HEAD], cos, sin).astype(BF)
        v_s[rows] = block[:, 2 * HEAD :].astype(BF)
        g_s[rows] = gm_ref[j, 0]
    for first in range(0, L, SPAN):
        last = first + SPAN
        q, g = q_s[first:last], g_s[first:last]
        k, v = k_s[:last], v_s[:last]
        row = lax.broadcasted_iota(jnp.int32, (SPAN, 1), 0) + first
        limit = row
        for piece in range(2):
            low = starts_ref[2 * m + piece]
            limit = jnp.where((row >= low) & (row < low + PIECE), low + PIECE - 1, limit)
        column = lax.broadcasted_iota(jnp.int32, (SPAN, last), 1)
        scores = jnp.where(column <= limit, contract_last(q, k) * scale, -jnp.inf)
        top = jnp.max(scores, axis=1, keepdims=True)
        powers = jnp.exp(scores - top)
        probs = powers * (1.0 / jnp.sum(powers, axis=1, keepdims=True))
        pb = probs.astype(BF)
        mix = mm(pb, v).astype(BF)
        gp = contract_last(g, v)
        delta = jnp.sum(gp * probs, axis=1, keepdims=True)
        gs = (probs * (gp - delta)).astype(BF)
        gq = mm(gs, k) * scale
        gk = contract_first(gs, q)
        gv = contract_first(pb, g)
        if first == 0:
            gk_s[:last] = gk
            gv_s[:last] = gv
            gk_s[last:] = jnp.zeros((L - last, HEAD), F32)
            gv_s[last:] = jnp.zeros((L - last, HEAD), F32)
        else:
            gk_s[:last] += gk
            gv_s[:last] += gv
        for a in range(first // part, last // part):
            rows = slice(a * part - first, (a + 1) * part - first)
            table = slice(a * part, (a + 1) * part)
            j = slot_ref[a]
            mix_ref[j, 0] = mix[rows]
            grad_ref[j, 0, :, :HEAD] = turn(gq[rows], cos_ref[table], -sin_ref[table]).astype(BF)
    for a in range(parts):
        rows = slice(a * part, (a + 1) * part)
        j = slot_ref[a]
        gk = gk_s[rows] * scale
        grad_ref[j, 0, :, HEAD : 2 * HEAD] = turn(gk, cos_ref[rows], -sin_ref[rows]).astype(BF)
        grad_ref[j, 0, :, 2 * HEAD :] = gv_s[rows].astype(BF)


def attention(slots, starts, merged_pre, grad_mix, tables, micro, parts):
    part = L // parts
    heads = merged_pre.shape[1] // (3 * HEAD)
    cos, sin = tables
    pre = merged_pre.reshape(parts, micro, part, heads * 3 * HEAD)
    gm = grad_mix.reshape(parts, micro, part, heads * HEAD)
    spec = lambda w: pl.BlockSpec((parts, 1, part, w), lambda h, m, *_: (0, m, 0, h))
    table = pl.BlockSpec((L, 128), lambda h, m, *_: (0, 0))
    flops = heads * micro * 2 * 5 * L * L * HEAD * 3 // 4
    mix, grads = pl.pallas_call(
        functools.partial(attention_kernel, parts=parts, part=part),
        out_shape=(
            jax.ShapeDtypeStruct(gm.shape, BF),
            jax.ShapeDtypeStruct(pre.shape, BF),
        ),
        grid_spec=pltpu.PrefetchScalarGridSpec(
            num_scalar_prefetch=2,
            grid=(heads, micro),
            in_specs=[spec(3 * HEAD), spec(HEAD), table, table],
            out_specs=[spec(HEAD), spec(3 * HEAD)],
            scratch_shapes=[pltpu.VMEM((L, HEAD), BF)] * 4 + [pltpu.VMEM((L, HEAD), F32)] * 2,
        ),
        compiler_params=pltpu.CompilerParams(
            dimension_semantics=("arbitrary", "arbitrary"), vmem_limit_bytes=60 << 20
        ),
        cost_estimate=pl.CostEstimate(
            flops=2 * flops, bytes_accessed=pre.size * 6 + gm.size * 4, transcendentals=heads * micro * L * L
        ),
        name="attention",
    )(slots, starts, pre, gm, cos, sin)
    return mix.reshape(-1, heads * HEAD), grads.reshape(-1, heads * 3 * HEAD)


def after(value, *earlier):
    return lax.optimization_barrier((value,) + earlier)[0]


def ring_order(rows):
    if rows < 4:
        return list(range(rows))
    half = rows // 2
    return list(range(half)) + list(range(rows - 1, half - 1, -1))


def body(
    inputs,
    piece_starts,
    first_gain,
    first_shift,
    second_gain,
    second_shift,
    merged_weight,
    merged_bias,
    output_weight,
    output_bias,
    expand_weight,
    expand_bias,
    reduce_weight,
    reduce_bias,
    cotangent,
):
    rows = lax.axis_size("row")
    cols = lax.axis_size("col")
    micro, own_tokens, width = inputs.shape
    per_row = own_tokens // L
    part = L // rows
    block_rows = micro * part
    order = ring_order(rows)
    spot = [order.index(r) for r in range(rows)]
    ahead = [(order[i], order[(i + 1) % rows]) for i in range(rows)]
    behind = [(b, a) for a, b in ahead]
    me = lax.axis_index("row")
    my_spot = jnp.asarray(spot, jnp.int32)[me]
    slots = (jnp.asarray(spot, jnp.int32) - my_spot) % rows
    up = lambda v: lax.ppermute(v, "row", ahead)
    down = lambda v: lax.ppermute(v, "row", behind)

    def row_swap(own):
        b = own.reshape(micro, per_row, rows, part, width).transpose(2, 1, 0, 3, 4)
        b = lax.all_to_all(b, "row", split_axis=0, concat_axis=0, tiled=True)
        return b.reshape(rows * per_row, block_rows, width)

    def col_swap(b):
        return lax.all_to_all(b, "col", split_axis=0, concat_axis=0, tiled=True)

    def side_by_side(b):
        return b.transpose(1, 0, 2).reshape(block_rows, cols * width)

    def from_rows(block, *earlier):
        b = block.reshape(rows, per_row, micro, part, width)
        if earlier:
            b = lax.all_to_all(after(b, *earlier), "row", split_axis=0, concat_axis=0, tiled=True)
            return b.transpose(2, 1, 0, 3, 4).reshape(micro, own_tokens, width)
        b = b.transpose(0, 2, 1, 3, 4)
        whole = jnp.zeros((micro, per_row, rows, part, width), BF)
        for step in range(rows):
            other = partner(me, step)
            source = me ^ step if rows & (rows - 1) == 0 else (me - step) % rows
            piece = lax.dynamic_index_in_dim(b, other, 0, keepdims=False)
            if step:
                piece = lax.ppermute(piece, "row", [(r, partner(r, step)) for r in range(rows)])
            whole = lax.dynamic_update_slice_in_dim(whole, piece[:, :, None], source, 2)
        return whole.reshape(micro, own_tokens, width)

    def partner(r, step):
        return r ^ step if rows & (rows - 1) == 0 else (r + step) % rows

    far = rows // 2
    cut = block_rows // 2

    def ring_gather(own, *earlier):
        pieces = [None] * rows
        pieces[0] = own
        fore, back = own, own
        for step in range(1, far):
            fore, back = up(fore), down(back)
            pieces[rows - step], pieces[step] = fore, back
        if earlier:
            fore, back = lax.optimization_barrier((fore, back) + earlier)[:2]
        pieces[far] = jnp.concatenate([up(fore[:cut]), down(back[cut:])], axis=0)
        return jnp.concatenate(pieces, axis=0)

    def chunk(total, j):
        return total[j * block_rows : (j + 1) * block_rows]

    def ring_open(total):
        last = chunk(total, far)
        return up(last[:cut]), down(last[cut:])

    def ring_close(total, halves):
        half_up, half_down = halves
        fore = back = None
        for step in range(far - 1, 0, -1):
            a, b = chunk(total, step).astype(F32), chunk(total, rows - step).astype(F32)
            if fore is None:
                a = jnp.concatenate([a[:cut] + half_up.astype(F32), a[cut:]], axis=0)
                b = jnp.concatenate([b[:cut], b[cut:] + half_down.astype(F32)], axis=0)
            else:
                a, b = a + fore.astype(F32), b + back.astype(F32)
            fore, back = up(a.astype(BF)), down(b.astype(BF))
        return chunk(total, 0).astype(F32) + fore.astype(F32) + back.astype(F32)

    def norm(block):
        block = block.astype(F32)
        center = jnp.mean(block, axis=-1, keepdims=True)
        spread = jnp.mean((block - center) ** 2, axis=-1, keepdims=True)
        inverse_std = lax.rsqrt(spread + norm_eps)
        return (block - center) * inverse_std, inverse_std

    def broadcast(value, axis, size):
        return lax.all_to_all(
            jnp.broadcast_to(value, (size,) + value.shape), axis, split_axis=0, concat_axis=0, tiled=True
        )

    gains = jnp.stack([first_gain, first_shift, second_gain, second_shift])
    spread_gains = broadcast(gains, "col", cols)
    gains = spread_gains.transpose(1, 0, 2).reshape(4, cols * width)
    expand_w = lax.all_gather(expand_weight, "col", axis=0, tiled=True)
    x_half = row_swap(after(inputs, spread_gains))
    cot_half = row_swap(after(cotangent, x_half))
    x_part = col_swap(after(x_half, cot_half))
    reduce_w = lax.all_gather(after(reduce_weight, x_part), "col", axis=1, tiled=True)
    mixed_weight = jnp.concatenate([merged_weight, output_weight.T], axis=1)
    cot_part = col_swap(after(cot_half, x_part))
    merged_cols = merged_weight.shape[1]
    x_part = side_by_side(x_part)
    x_seq = ring_gather(x_part)

    normed, _ = norm(x_seq)
    attend_in = (normed * gains[0] + gains[1]).astype(BF)
    expand_in = (normed * gains[2] + gains[3]).astype(BF)

    expand_pre = lax.optimization_barrier(mm(expand_in, expand_w) + expand_bias)
    cot_part = side_by_side(after(cot_part, expand_pre[:8, :128]))
    mixed_w = lax.all_gather(after(mixed_weight, cot_part), "col", axis=0, tiled=True)
    merged_w, output_wt = mixed_w[:, :merged_cols], mixed_w[:, merged_cols:]
    phi_sum = 0.5 * (1.0 + lax.erf(expand_pre * (0.5 ** 0.5)))
    density = jnp.exp(-0.5 * expand_pre * expand_pre) * 0.3989422804014327
    activated = (expand_pre * phi_sum).astype(BF)
    slope = (phi_sum + expand_pre * density).astype(BF)
    activated, slope = lax.optimization_barrier((activated, slope))
    branch_ff = mm(activated, reduce_w).astype(BF)
    cot_seq = ring_gather(cot_part, branch_ff)

    def scatter_weight(grad):
        return lax.psum_scatter(grad, "col", scatter_dimension=0, tiled=True)

    cot_seq, branch_ff, attend_in, *tables = lax.optimization_barrier(
        (cot_seq, branch_ff, attend_in) + rotary_tables()
    )
    reduce_dot = contract_first(cot_seq, activated).astype(BF)
    reduce_grad = scatter_weight(reduce_dot)
    grad_act = contract_last(after(cot_seq, reduce_dot), reduce_w)
    grad_pre = (grad_act * slope.astype(F32)).astype(BF)
    expand_b = jnp.sum(grad_pre.astype(F32), axis=0)
    expand_dot = contract_first(expand_in, grad_pre).astype(BF)
    expand_grad = scatter_weight(expand_dot)

    merged_pre = mm(after(attend_in, expand_dot), merged_w) + merged_bias
    grad_mix = mm(after(cot_seq, expand_dot), output_wt).astype(BF)
    mix, grad_merged = attention(
        slots, piece_starts.reshape(-1), merged_pre, grad_mix, tables, micro, rows
    )
    branch = (contract_last(mix, output_wt) + branch_ff).astype(BF)
    halves = ring_open(branch)
    grad_merged, attend_late = lax.optimization_barrier(
        (grad_merged, attend_in, branch, reduce_grad)
    )[:2]
    merged_dot = contract_first(attend_late, grad_merged).astype(BF)
    merged_grad = scatter_weight(merged_dot)
    grad_merged, grad_pre, half_up, half_down = lax.optimization_barrier(
        (grad_merged, grad_pre) + halves + (merged_dot,)
    )[:4]
    branch = ring_close(branch, (half_up, half_down))
    grad_first = contract_last(grad_merged, merged_w)
    grad_second = contract_last(grad_pre, expand_w)
    norm_sums = jnp.stack(
        [
            jnp.sum(grad_first * normed, axis=0),
            jnp.sum(grad_first, axis=0),
            jnp.sum(grad_second * normed, axis=0),
            jnp.sum(grad_second, axis=0),
        ]
    )
    grad_hat = (grad_first * gains[0] + grad_second * gains[2]).astype(BF)
    halves = ring_open(grad_hat)
    merged_b = jnp.sum(grad_merged.astype(F32), axis=0)
    shift_b = jnp.sum(cotangent.astype(F32), axis=(0, 1))
    sums = jnp.concatenate(
        [
            norm_sums.reshape(4, cols, width).transpose(1, 0, 2).reshape(cols, 4 * width),
            jnp.broadcast_to(merged_b, (cols, merged_cols)),
            jnp.broadcast_to(expand_b, (cols, expand_b.shape[0])),
        ],
        axis=1,
    ).reshape(cols, -1, 128)
    branch = col_swap(branch.astype(BF).reshape(block_rows, cols, width).transpose(1, 0, 2))
    spread_sums = lax.all_to_all(
        after(sums, branch), "col", split_axis=0, concat_axis=0, tiled=True
    )
    halves = lax.optimization_barrier(halves + (expand_grad,))[:2]
    grad_hat = ring_close(grad_hat, halves)
    sums = jnp.sum(spread_sums.reshape(cols, -1), axis=0)
    merged_b = sums[4 * width : 4 * width + merged_cols]
    expand_b = sums[4 * width + merged_cols :]
    tail = jnp.concatenate([sums[: 4 * width], shift_b]).reshape(-1, 128)
    if rows & (rows - 1) == 0:
        step = 1
        while step < rows:
            far_tail = lax.ppermute(tail, "row", [(r, r ^ step) for r in range(rows)])
            tail = tail + far_tail
            step *= 2
    else:
        far_tail = broadcast(tail, "row", rows)
        tail = jnp.sum(far_tail, axis=0)
    tail = tail.reshape(5, width)
    branch = from_rows(branch)
    result = inputs.astype(F32) + branch.astype(F32) + output_bias + reduce_bias
    result = result.astype(BF)

    part_normed, part_inverse = norm(x_part)
    norm_part = part_inverse * (
        grad_hat
        - jnp.mean(grad_hat, axis=-1, keepdims=True)
        - part_normed * jnp.mean(grad_hat * part_normed, axis=-1, keepdims=True)
    )

    norm_part = after(norm_part.astype(BF), merged_grad, spread_sums)
    norm_part = col_swap(norm_part.reshape(block_rows, cols, width).transpose(1, 0, 2))
    mix_late, cot_late = lax.optimization_barrier((mix, cot_seq, grad_hat, far_tail))[:2]
    output_dot = contract_first(cot_late, mix_late).astype(BF)
    output_grad = scatter_weight(after(output_dot, norm_part))
    input_grad = cotangent.astype(F32) + from_rows(norm_part, result, output_dot).astype(F32)
    norm_sums, shift_b = tail[:4], tail[4]
    return (
        result,
        input_grad,
        norm_sums[0],
        norm_sums[1],
        norm_sums[2],
        norm_sums[3],
        merged_grad.astype(F32),
        merged_b,
        output_grad.T.astype(F32),
        shift_b,
        expand_grad.astype(F32),
        expand_b,
        reduce_grad.T.astype(F32),
        shift_b,
    )


def solution(mesh):
    in_specs = (
        P(None, "row", "col"),
        P(None, "col", None),
        P("col"),
        P("col"),
        P("col"),
        P("col"),
        P("col", "row"),
        P("row"),
        P("row", "col"),
        P("col"),
        P("col", "row"),
        P("row"),
        P("row", "col"),
        P("col"),
        P(None, "row", "col"),
    )
    out_specs = (
        P(None, "row", "col"),
        P(None, "row", "col"),
        P("col"),
        P("col"),
        P("col"),
        P("col"),
        P("col", "row"),
        P("row"),
        P("row", "col"),
        P("col"),
        P("col", "row"),
        P("row"),
        P("row", "col"),
        P("col"),
    )
    return jax.shard_map(body, mesh=mesh, in_specs=in_specs, out_specs=out_specs, check_vma=False)
```

```python
import functools

import jax
import jax.numpy as jnp
from jax import lax
from jax.experimental import pallas as pl
from jax.experimental.pallas import tpu as pltpu
from jax.sharding import PartitionSpec as P

D = 2048
HEAD = 256
ROT = 64
L = 1024
PIECE = 256
SPAN = 512

norm_eps = 1e-05
theta_base = 10000.0
BF = jnp.bfloat16
F32 = jnp.float32


def mm(left, right):
    return jnp.dot(left, right, preferred_element_type=F32)


def contract_last(left, right):
    return lax.dot_general(left, right, (((1,), (1,)), ((), ())), preferred_element_type=F32)


def contract_first(left, right):
    return lax.dot_general(left, right, (((0,), (0,)), ((), ())), preferred_element_type=F32)


def rotary_tables():
    half = ROT // 2
    freq_steps = jnp.arange(half, dtype=F32)
    inverse = jnp.power(theta_base, -(2.0 * freq_steps) / ROT)
    angles = jnp.arange(L, dtype=jnp.int32).astype(F32)[:, None] * inverse[None, :]
    cosine = jnp.cos(angles)
    sine = jnp.sin(angles)
    rest = 128 - ROT
    cos_table = jnp.concatenate([cosine, cosine, jnp.ones((L, rest), F32)], axis=1)
    sin_table = jnp.concatenate([-sine, sine, jnp.zeros((L, rest), F32)], axis=1)
    return cos_table, sin_table


def turn(block, cos, sin):
    half = ROT // 2
    head = block[:, :128]
    lane = lax.broadcasted_iota(jnp.int32, head.shape, 1)
    partner = jnp.where(lane < half, pltpu.roll(head, 128 - half, 1), pltpu.roll(head, half, 1))
    return jnp.concatenate([head * cos + partner * sin, block[:, 128:]], axis=1)


def attention_kernel(
    slot_ref, starts_ref, pre_ref, gm_ref, cos_ref, sin_ref,
    mix_ref, grad_ref, q_s, k_s, v_s, g_s, gk_s, gv_s, *, parts, part,
):
    m = pl.program_id(1)
    scale = HEAD ** (-0.5)
    for a in range(parts):
        rows = slice(a * part, (a + 1) * part)
        j = slot_ref[a]
        block = pre_ref[j, 0]
        cos, sin = cos_ref[rows], sin_ref[rows]
        q_s[rows] = turn(block[:, :HEAD], cos, sin).astype(BF)
        k_s[rows] = turn(block[:, HEAD : 2 * HEAD], cos, sin).astype(BF)
        v_s[rows] = block[:, 2 * HEAD :].astype(BF)
        g_s[rows] = gm_ref[j, 0]
    for first in range(0, L, SPAN):
        last = first + SPAN
        q, g = q_s[first:last], g_s[first:last]
        k, v = k_s[:last], v_s[:last]
        row = lax.broadcasted_iota(jnp.int32, (SPAN, 1), 0) + first
        limit = row
        for piece in range(2):
            low = starts_ref[2 * m + piece]
            limit = jnp.where((row >= low) & (row < low + PIECE), low + PIECE - 1, limit)
        column = lax.broadcasted_iota(jnp.int32, (SPAN, last), 1)
        scores = jnp.where(column <= limit, contract_last(q, k) * scale, -jnp.inf)
        top = jnp.max(scores, axis=1, keepdims=True)
        powers = jnp.exp(scores - top)
        probs = powers * (1.0 / jnp.sum(powers, axis=1, keepdims=True))
        pb = probs.astype(BF)
        mix = mm(pb, v).astype(BF)
        gp = contract_last(g, v)
        delta = jnp.sum(gp * probs, axis=1, keepdims=True)
        gs = (probs * (gp - delta)).astype(BF)
        gq = mm(gs, k) * scale
        gk = contract_first(gs, q)
        gv = contract_first(pb, g)
        if first == 0:
            gk_s[:last] = gk
            gv_s[:last] = gv
            gk_s[last:] = jnp.zeros((L - last, HEAD), F32)
            gv_s[last:] = jnp.zeros((L - last, HEAD), F32)
        else:
            gk_s[:last] += gk
            gv_s[:last] += gv
        for a in range(first // part, last // part):
            rows = slice(a * part - first, (a + 1) * part - first)
            table = slice(a * part, (a + 1) * part)
            j = slot_ref[a]
            mix_ref[j, 0] = mix[rows]
            grad_ref[j, 0, :, :HEAD] = turn(gq[rows], cos_ref[table], -sin_ref[table]).astype(BF)
    for a in range(parts):
        rows = slice(a * part, (a + 1) * part)
        j = slot_ref[a]
        gk = gk_s[rows] * scale
        grad_ref[j, 0, :, HEAD : 2 * HEAD] = turn(gk, cos_ref[rows], -sin_ref[rows]).astype(BF)
        grad_ref[j, 0, :, 2 * HEAD :] = gv_s[rows].astype(BF)


def attention(slots, starts, merged_pre, grad_mix, tables, micro, parts):
    part = L // parts
    heads = merged_pre.shape[1] // (3 * HEAD)
    cos, sin = tables
    pre = merged_pre.reshape(parts, micro, part, heads * 3 * HEAD)
    gm = grad_mix.reshape(parts, micro, part, heads * HEAD)
    spec = lambda w: pl.BlockSpec((parts, 1, part, w), lambda h, m, *_: (0, m, 0, h))
    table = pl.BlockSpec((L, 128), lambda h, m, *_: (0, 0))
    flops = heads * micro * 2 * 5 * L * L * HEAD * 3 // 4
    mix, grads = pl.pallas_call(
        functools.partial(attention_kernel, parts=parts, part=part),
        out_shape=(
            jax.ShapeDtypeStruct(gm.shape, BF),
            jax.ShapeDtypeStruct(pre.shape, BF),
        ),
        grid_spec=pltpu.PrefetchScalarGridSpec(
            num_scalar_prefetch=2,
            grid=(heads, micro),
            in_specs=[spec(3 * HEAD), spec(HEAD), table, table],
            out_specs=[spec(HEAD), spec(3 * HEAD)],
            scratch_shapes=[pltpu.VMEM((L, HEAD), BF)] * 4 + [pltpu.VMEM((L, HEAD), F32)] * 2,
        ),
        compiler_params=pltpu.CompilerParams(
            dimension_semantics=("arbitrary", "arbitrary"), vmem_limit_bytes=60 << 20
        ),
        cost_estimate=pl.CostEstimate(
            flops=2 * flops, bytes_accessed=pre.size * 6 + gm.size * 4, transcendentals=heads * micro * L * L
        ),
        name="attention",
    )(slots, starts, pre, gm, cos, sin)
    return mix.reshape(-1, heads * HEAD), grads.reshape(-1, heads * 3 * HEAD)


def after(value, *earlier):
    return lax.optimization_barrier((value,) + earlier)[0]


def ring_order(rows):
    if rows < 4:
        return list(range(rows))
    half = rows // 2
    return list(range(half)) + list(range(rows - 1, half - 1, -1))


def body(
    inputs,
    piece_starts,
    first_gain,
    first_shift,
    second_gain,
    second_shift,
    merged_weight,
    merged_bias,
    output_weight,
    output_bias,
    expand_weight,
    expand_bias,
    reduce_weight,
    reduce_bias,
    cotangent,
):
    rows = lax.axis_size("row")
    cols = lax.axis_size("col")
    micro, own_tokens, width = inputs.shape
    per_row = own_tokens // L
    part = L // rows
    block_rows = micro * part
    order = ring_order(rows)
    spot = [order.index(r) for r in range(rows)]
    ahead = [(order[i], order[(i + 1) % rows]) for i in range(rows)]
    behind = [(b, a) for a, b in ahead]
    me = lax.axis_index("row")
    my_spot = jnp.asarray(spot, jnp.int32)[me]
    slots = (jnp.asarray(spot, jnp.int32) - my_spot) % rows
    up = lambda v: lax.ppermute(v, "row", ahead)
    down = lambda v: lax.ppermute(v, "row", behind)

    def row_swap(own):
        b = own.reshape(micro, per_row, rows, part, width).transpose(2, 1, 0, 3, 4)
        b = lax.all_to_all(b, "row", split_axis=0, concat_axis=0, tiled=True)
        return b.reshape(rows * per_row, block_rows, width)

    def col_swap(b):
        return lax.all_to_all(b, "col", split_axis=0, concat_axis=0, tiled=True)

    def side_by_side(b):
        return b.transpose(1, 0, 2).reshape(block_rows, cols * width)

    def from_rows(block, *earlier):
        b = block.reshape(rows, per_row, micro, part, width)
        if earlier:
            b = lax.all_to_all(after(b, *earlier), "row", split_axis=0, concat_axis=0, tiled=True)
            return b.transpose(2, 1, 0, 3, 4).reshape(micro, own_tokens, width)
        b = b.transpose(0, 2, 1, 3, 4)
        whole = jnp.zeros((micro, per_row, rows, part, width), BF)
        for step in range(rows):
            other = partner(me, step)
            source = me ^ step if rows & (rows - 1) == 0 else (me - step) % rows
            piece = lax.dynamic_index_in_dim(b, other, 0, keepdims=False)
            if step:
                piece = lax.ppermute(piece, "row", [(r, partner(r, step)) for r in range(rows)])
            whole = lax.dynamic_update_slice_in_dim(whole, piece[:, :, None], source, 2)
        return whole.reshape(micro, own_tokens, width)

    def partner(r, step):
        return r ^ step if rows & (rows - 1) == 0 else (r + step) % rows

    far = rows // 2
    cut = block_rows // 2

    def ring_gather(own, *earlier):
        pieces = [None] * rows
        pieces[0] = own
        fore, back = own, own
        for step in range(1, far):
            fore, back = up(fore), down(back)
            pieces[rows - step], pieces[step] = fore, back
        if earlier:
            fore, back = lax.optimization_barrier((fore, back) + earlier)[:2]
        pieces[far] = jnp.concatenate([up(fore[:cut]), down(back[cut:])], axis=0)
        return jnp.concatenate(pieces, axis=0)

    def chunk(total, j):
        return total[j * block_rows : (j + 1) * block_rows]

    def ring_open(total):
        last = chunk(total, far)
        return up(last[:cut]), down(last[cut:])

    def ring_close(total, halves):
        half_up, half_down = halves
        fore = back = None
        for step in range(far - 1, 0, -1):
            a, b = chunk(total, step).astype(F32), chunk(total, rows - step).astype(F32)
            if fore is None:
                a = jnp.concatenate([a[:cut] + half_up.astype(F32), a[cut:]], axis=0)
                b = jnp.concatenate([b[:cut], b[cut:] + half_down.astype(F32)], axis=0)
            else:
                a, b = a + fore.astype(F32), b + back.astype(F32)
            fore, back = up(a.astype(BF)), down(b.astype(BF))
        return chunk(total, 0).astype(F32) + fore.astype(F32) + back.astype(F32)

    def norm(block):
        block = block.astype(F32)
        center = jnp.mean(block, axis=-1, keepdims=True)
        spread = jnp.mean((block - center) ** 2, axis=-1, keepdims=True)
        inverse_std = lax.rsqrt(spread + norm_eps)
        return (block - center) * inverse_std, inverse_std

    def broadcast(value, axis, size):
        return lax.all_to_all(
            jnp.broadcast_to(value, (size,) + value.shape), axis, split_axis=0, concat_axis=0, tiled=True
        )

    gains = jnp.stack([first_gain, first_shift, second_gain, second_shift])
    if cols & (cols - 1):
        spread_gains = broadcast(gains, "col", cols)
    else:
        mine = lax.broadcasted_iota(jnp.int32, (cols, 1, 1), 0) == lax.axis_index("col")
        spread_gains = jnp.where(mine, gains[None], 0.0)
        step = 1
        while step < cols:
            spread_gains += lax.ppermute(spread_gains, "col", [(c, c ^ step) for c in range(cols)])
            step *= 2
    gains = spread_gains.transpose(1, 0, 2).reshape(4, cols * width)
    expand_w = lax.all_gather(expand_weight, "col", axis=0, tiled=True)
    x_half = row_swap(inputs)
    cot_half = row_swap(after(cotangent, x_half))
    x_part = col_swap(after(x_half, cot_half, spread_gains))
    reduce_w = lax.all_gather(after(reduce_weight, x_part), "col", axis=1, tiled=True)
    mixed_weight = jnp.concatenate([merged_weight, output_weight.T], axis=1)
    cot_part = col_swap(after(cot_half, x_part))
    merged_cols = merged_weight.shape[1]
    x_part = side_by_side(x_part)
    x_seq = ring_gather(x_part)

    normed, _ = norm(x_seq)
    attend_in = (normed * gains[0] + gains[1]).astype(BF)
    expand_in = (normed * gains[2] + gains[3]).astype(BF)

    expand_pre = lax.optimization_barrier(mm(expand_in, expand_w) + expand_bias)
    cot_part = side_by_side(after(cot_part, expand_pre[:8, :128]))
    mixed_w = lax.all_gather(after(mixed_weight, cot_part), "col", axis=0, tiled=True)
    merged_w, output_wt = mixed_w[:, :merged_cols], mixed_w[:, merged_cols:]
    phi_sum = 0.5 * (1.0 + lax.erf(expand_pre * (0.5 ** 0.5)))
    density = jnp.exp(-0.5 * expand_pre * expand_pre) * 0.3989422804014327
    activated = (expand_pre * phi_sum).astype(BF)
    slope = (phi_sum + expand_pre * density).astype(BF)
    activated, slope = lax.optimization_barrier((activated, slope))
    branch_ff = mm(activated, reduce_w).astype(BF)
    cot_seq = ring_gather(cot_part, branch_ff)

    def scatter_weight(grad):
        return lax.psum_scatter(grad, "col", scatter_dimension=0, tiled=True)

    cot_seq, branch_ff, attend_in, *tables = lax.optimization_barrier(
        (cot_seq, branch_ff, attend_in) + rotary_tables()
    )
    reduce_dot = contract_first(cot_seq, activated).astype(BF)
    reduce_grad = scatter_weight(reduce_dot)
    grad_act = contract_last(after(cot_seq, reduce_dot), reduce_w)
    grad_pre = (grad_act * slope.astype(F32)).astype(BF)
    expand_b = jnp.sum(grad_pre.astype(F32), axis=0)
    expand_dot = contract_first(expand_in, grad_pre).astype(BF)
    expand_grad = scatter_weight(expand_dot)

    merged_pre = mm(after(attend_in, expand_dot), merged_w) + merged_bias
    grad_mix = mm(after(cot_seq, expand_dot), output_wt).astype(BF)
    mix, grad_merged = attention(
        slots, piece_starts.reshape(-1), merged_pre, grad_mix, tables, micro, rows
    )
    branch = (contract_last(mix, output_wt) + branch_ff).astype(BF)
    halves = ring_open(branch)
    grad_merged, attend_late = lax.optimization_barrier(
        (grad_merged, attend_in, branch, reduce_grad)
    )[:2]
    merged_dot = contract_first(attend_late, grad_merged).astype(BF)
    merged_grad = scatter_weight(merged_dot)
    grad_merged, grad_pre, half_up, half_down = lax.optimization_barrier(
        (grad_merged, grad_pre) + halves + (merged_dot,)
    )[:4]
    branch = ring_close(branch, (half_up, half_down))
    grad_first = contract_last(grad_merged, merged_w)
    grad_second = contract_last(grad_pre, expand_w)
    norm_sums = jnp.stack(
        [
            jnp.sum(grad_first * normed, axis=0),
            jnp.sum(grad_first, axis=0),
            jnp.sum(grad_second * normed, axis=0),
            jnp.sum(grad_second, axis=0),
        ]
    )
    grad_hat = (grad_first * gains[0] + grad_second * gains[2]).astype(BF)
    halves = ring_open(grad_hat)
    merged_b = jnp.sum(grad_merged.astype(F32), axis=0)
    shift_b = jnp.sum(cotangent.astype(F32), axis=(0, 1))
    sums = jnp.concatenate(
        [
            norm_sums.reshape(4, cols, width).transpose(1, 0, 2).reshape(cols, 4 * width),
            jnp.broadcast_to(merged_b, (cols, merged_cols)),
            jnp.broadcast_to(expand_b, (cols, expand_b.shape[0])),
        ],
        axis=1,
    ).reshape(cols, -1, 128)
    branch = col_swap(branch.astype(BF).reshape(block_rows, cols, width).transpose(1, 0, 2))
    spread_sums = lax.all_to_all(
        after(sums, branch), "col", split_axis=0, concat_axis=0, tiled=True
    )
    halves = lax.optimization_barrier(halves + (expand_grad,))[:2]
    grad_hat = ring_close(grad_hat, halves)
    sums = jnp.sum(spread_sums.reshape(cols, -1), axis=0)
    merged_b = sums[4 * width : 4 * width + merged_cols]
    expand_b = sums[4 * width + merged_cols :]
    tail = jnp.concatenate([sums[: 4 * width], shift_b]).reshape(-1, 128)
    if rows & (rows - 1) == 0:
        step = 1
        while step < rows:
            far_tail = lax.ppermute(tail, "row", [(r, r ^ step) for r in range(rows)])
            tail = tail + far_tail
            step *= 2
    else:
        far_tail = broadcast(tail, "row", rows)
        tail = jnp.sum(far_tail, axis=0)
    tail = tail.reshape(5, width)
    branch = from_rows(branch)
    result = inputs.astype(F32) + branch.astype(F32) + output_bias + reduce_bias
    result = result.astype(BF)

    part_normed, part_inverse = norm(x_part)
    norm_part = part_inverse * (
        grad_hat
        - jnp.mean(grad_hat, axis=-1, keepdims=True)
        - part_normed * jnp.mean(grad_hat * part_normed, axis=-1, keepdims=True)
    )

    norm_part = after(norm_part.astype(BF), merged_grad, spread_sums)
    norm_part = col_swap(norm_part.reshape(block_rows, cols, width).transpose(1, 0, 2))
    mix_late, cot_late = lax.optimization_barrier((mix, cot_seq, grad_hat, far_tail))[:2]
    output_dot = contract_first(cot_late, mix_late).astype(BF)
    output_grad = scatter_weight(after(output_dot, norm_part))
    input_grad = cotangent.astype(F32) + from_rows(norm_part, result, output_dot).astype(F32)
    norm_sums, shift_b = tail[:4], tail[4]
    return (
        result,
        input_grad,
        norm_sums[0],
        norm_sums[1],
        norm_sums[2],
        norm_sums[3],
        merged_grad.astype(F32),
        merged_b,
        output_grad.T.astype(F32),
        shift_b,
        expand_grad.astype(F32),
        expand_b,
        reduce_grad.T.astype(F32),
        shift_b,
    )


def solution(mesh):
    in_specs = (
        P(None, "row", "col"),
        P(None, "col", None),
        P("col"),
        P("col"),
        P("col"),
        P("col"),
        P("col", "row"),
        P("row"),
        P("row", "col"),
        P("col"),
        P("col", "row"),
        P("row"),
        P("row", "col"),
        P("col"),
        P(None, "row", "col"),
    )
    out_specs = (
        P(None, "row", "col"),
        P(None, "row", "col"),
        P("col"),
        P("col"),
        P("col"),
        P("col"),
        P("col", "row"),
        P("row"),
        P("row", "col"),
        P("col"),
        P("col", "row"),
        P("row"),
        P("row", "col"),
        P("col"),
    )
    return jax.shard_map(body, mesh=mesh, in_specs=in_specs, out_specs=out_specs, check_vma=False)
```
